256 devices in a mesh: gx: 16 (over z, core), gy: 16 (over y, x).
Axes of the slice: x: 4, y: 4, z: 8, core: 2. Of those that a mesh axis runs over, the one named last changes fastest.
Arguments:
- populations: float32 [19, 8, 128, 2048], P(None, None, 'gy', 'gx'), may hold values from 0.49 to 22.2, as said below
- concentrations: float32 [3, 8, 128, 2048], P(None, None, 'gy', 'gx'), may hold values from 0.5 to 2
- potential: float32 [8, 128, 2048], P(None, 'gy', 'gx'), may hold values from -5 to 5
- solid_mask: int32 [8, 128, 2048], P(None, 'gy', 'gx'), may hold values 0 or 1
- surface_sign: int32 [8, 128, 2048], P(None, 'gy', 'gx'), may hold values from -1 to 1
Outputs:
- populations_new: float32 [19, 8, 128, 2048], P(None, None, 'gy', 'gx')
- concentrations_new: float32 [3, 8, 128, 2048], P(None, None, 'gy', 'gx')
- potential_new: float32 [8, 128, 2048], P(None, 'gy', 'gx')
The draws below stay inside these ranges and needn't reach their ends.
Inputs may be any that keep to these rules, and one draw needn't show every extreme that they name: `populations`: every entry is positive, near 36 times the weight of its velocity times a density of order one. `solid_mask`: 1 marks a solid cell, 0 a fluid one. `surface_sign`: read only at solid cells.
All inputs are finite; a program needn't handle non-finite values. No bound on the sum of `solid_mask` on one device may be relied on, other than what follows from the above.
Results may differ from the reference program's by a relative error of at most 0.0018.
Values sent between devices are 32-bit elements; how exact they have to be, the bound alone decides.
No kernel may reach another device: no remote copies, remote signals or barrier semaphores. Data moves between devices by JAX's collectives and lax.ppermute only.
A program may use at most 64 MiB of HBM per device.

```python
import math
import jax
import jax.numpy as jnp
import numpy as np
from jax import lax

NZ = 8
SPECIES = 3
STEPS = 4
CYCLES = 2
SSTEP = 4
NX = 2048
NY = 128


lattice_weight = (1.0 / 3.0,) + (1.0 / 18.0,) * 6 + (1.0 / 36.0,) * 12


def draw_populations(key, part):
    weights_col = jnp.array(lattice_weight, jnp.float32).reshape(19, 1, 1, 1)
    noise = jax.random.uniform(key, (19, NZ, NY, NX), jnp.float32, -0.3, 0.3)
    return 36.0 * weights_col * (1.0 + noise)


def with_ends(entries, key, low, largest):
    place = [jax.random.randint(jax.random.fold_in(key, axis), (), 0, length) for axis, length in enumerate(entries.shape)]
    longest = entries.shape.index(max(entries.shape))
    beside = place[:longest] + [(place[longest] + 1) % entries.shape[longest]] + place[longest + 1:]
    return entries.at[tuple(place)].set(low).at[tuple(beside)].set(largest)


def shard_levels(stream_key, shape, pieces, low, top_value):
    gain, own = 1.0, jax.random.fold_in(stream_key, 6)
    for position, parts in pieces:
        steps = jnp.exp(jax.random.uniform(jax.random.fold_in(own, position), (parts,), jnp.float32, low / len(pieces), top_value / len(pieces)))
        gain = gain * jnp.repeat(steps, shape[position] // parts).reshape([-1 if axis == position else 1 for axis in range(len(shape))])
    return gain


def normal_values(stream_key, shape, spread, reach, pieces=(), dtype=jnp.bfloat16):
    values = jax.random.normal(stream_key, shape, jnp.float32) * spread
    if len(pieces) > 0:
        values = shard_levels(stream_key, shape, pieces, -0.22, 0.18) * values
    return jnp.clip(values, min=-reach, max=reach).astype(dtype)


def setup_inputs(seed: int = 0) -> dict:
    splits = jax.random.split(jax.random.key(seed), 6)
    populations = draw_populations(jax.random.fold_in(splits[5], 71), 0)
    concentrations = jnp.clip(jnp.exp(math.log(2.0) - 1.3862944 * jax.random.uniform(splits[1], (SPECIES, NZ, NY, NX), jnp.float32) ** shard_levels(splits[1], (SPECIES, NZ, NY, NX), ((2, 16), (3, 16)), -0.2, 0.2)), 0.5, 2.0)
    potential = normal_values(splits[2], (NZ, NY, NX), 1.0, 5.0, ((1, 16), (2, 16)), jnp.float32)
    solid_mask = with_ends((jax.random.randint(splits[3], (NZ, NY, NX), 0, 8) < 1).astype(jnp.int32), jax.random.fold_in(splits[3], 1), 0, 1)
    surface_sign = with_ends(jax.random.randint(splits[4], (NZ, NY, NX), -1, 2), jax.random.fold_in(splits[4], 1), -1, 1).astype(jnp.int32)
    return {"populations": populations, "concentrations": concentrations, "potential": potential, "solid_mask": solid_mask, "surface_sign": surface_sign}


lattice_velocity = ((0, 0, 0), (0, 0, 1), (0, 0, -1), (0, 1, 0), (0, -1, 0), (1, 0, 0), (-1, 0, 0),
                    (0, 1, 1), (0, -1, -1), (0, 1, -1), (0, -1, 1), (1, 0, 1), (-1, 0, -1), (1, 0, -1), (-1, 0, 1),
                    (1, 1, 0), (-1, -1, 0), (1, -1, 0), (-1, 1, 0))
opposite = (0, 2, 1, 4, 3, 6, 5, 8, 7, 10, 9, 12, 11, 14, 13, 16, 15, 18, 17)
lattice_weight = (1.0 / 3.0,) + (1.0 / 18.0,) * 6 + (1.0 / 36.0,) * 12
relax_time = 1.25
force_scale = 0.05
valences = (1.0, -1.0, 2.0)
diffusivity = (0.05, 0.07, 0.03)
diag_coef = 6.0001
surface_scale = 2.0


def lattice_dot(direction, vector):
    running = None
    for axis_id in range(3):
        if direction[axis_id] != 0:
            addend = vector[axis_id] if direction[axis_id] > 0 else -vector[axis_id]
            running = addend if running is None else running + addend
    return running


def ion_charge(concentration):
    return valences[0] * concentration[0] + valences[1] * concentration[1] + valences[2] * concentration[2]


def collide_cells(fields, concentration, fluid_mask, efield):
    density = fields[0]
    for member in range(1, 19):
        density = density + fields[member]
    momentum = []
    for axis_id in range(3):
        running = None
        for member in range(19):
            sign_val = lattice_velocity[member][axis_id]
            if sign_val != 0:
                addend = fields[member] if sign_val > 0 else -fields[member]
                running = addend if running is None else running + addend
        momentum.append(running)
    charge = fluid_mask * ion_charge(concentration)
    forcing = [force_scale * charge * efield[axis_id] for axis_id in range(3)]
    velocity = [(momentum[axis_id] + 0.5 * forcing[axis_id]) / density for axis_id in range(3)]
    speed_sq = velocity[0] * velocity[0] + velocity[1] * velocity[1] + velocity[2] * velocity[2]
    work_rate = velocity[0] * forcing[0] + velocity[1] * forcing[1] + velocity[2] * forcing[2]
    relaxed = []
    for member in range(19):
        weight = lattice_weight[member]
        if member == 0:
            projected = jnp.zeros_like(density)
            along_force = jnp.zeros_like(density)
        else:
            projected = lattice_dot(lattice_velocity[member], velocity)
            along_force = lattice_dot(lattice_velocity[member], forcing)
        balance = weight * density * (1.0 + 3.0 * projected + 4.5 * projected * projected - 1.5 * speed_sq)
        source = weight * (3.0 * (along_force - work_rate) + 9.0 * projected * along_force)
        relaxed.append(fields[member] - (fields[member] - balance) / relax_time + (1.0 - 0.5 / relax_time) * source)
    return relaxed, velocity


def face_flux(low, high, pot_low, pot_high, vel_low, vel_high, opened):
    rates = jnp.array(diffusivity, jnp.float32).reshape(3, 1, 1, 1)
    drift = jnp.array(valences, jnp.float32).reshape(3, 1, 1, 1) * rates
    middle = 0.5 * (low + high)
    return opened * (-rates * (high - low) - drift * middle * (pot_high - pot_low) + 0.5 * (vel_low + vel_high) * middle)


def ion_update(concentration, potential, velocity, fluid_mask):
    running = None
    for axis_id in range(3):
        fluxes = face_flux(concentration, jnp.roll(concentration, -1, axis_id + 1), potential,
                           jnp.roll(potential, -1, axis_id), velocity[axis_id], jnp.roll(velocity[axis_id], -1, axis_id),
                           fluid_mask * jnp.roll(fluid_mask, -1, axis_id))
        change = fluxes - jnp.roll(fluxes, 1, axis_id + 1)
        running = change if running is None else running + change
    return concentration - running


def neighbor_sum(stack):
    return ((jnp.roll(stack, -1, 1) + jnp.roll(stack, 1, 1)) + (jnp.roll(stack, -1, 2) + jnp.roll(stack, 1, 2))
            + (jnp.roll(stack, -1, 3) + jnp.roll(stack, 1, 3)))


def next_level(summed, previous):
    if previous is None:
        return -summed / 6.0
    return -summed / 3.0 - previous


def shift_table():
    order_m = 2 * SSTEP + 1
    coeffs = np.zeros((order_m, order_m), np.float32)
    for block_start in (0, SSTEP + 1):
        block_depth = SSTEP if block_start == 0 else SSTEP - 1
        for column in range(block_depth):
            coeffs[block_start + column, block_start + column] = diag_coef
            coeffs[block_start + column + 1, block_start + column] = 6.0 if column == 0 else 3.0
            if column > 0:
                coeffs[block_start + column - 1, block_start + column] = 3.0
    return coeffs


def krylov_steps(gram_matrix):
    order_m = 2 * SSTEP + 1
    highest = lax.Precision.HIGHEST
    coeffs = jnp.asarray(shift_table(), jnp.float32)
    search_co = jnp.zeros((order_m,), jnp.float32).at[0].set(1.0)
    resid_co = jnp.zeros((order_m,), jnp.float32).at[SSTEP + 1].set(1.0)
    sol_co = jnp.zeros((order_m,), jnp.float32)
    residual_sq = jnp.dot(resid_co, jnp.dot(gram_matrix, resid_co, precision=highest), precision=highest)
    for inner_id in range(SSTEP):
        image_co = jnp.dot(coeffs, search_co, precision=highest)
        step_len = residual_sq / jnp.dot(search_co, jnp.dot(gram_matrix, image_co, precision=highest), precision=highest)
        sol_co = sol_co + step_len * search_co
        resid_co = resid_co - step_len * image_co
        fresh_sq = jnp.dot(resid_co, jnp.dot(gram_matrix, resid_co, precision=highest), precision=highest)
        search_co = resid_co + (fresh_sq / residual_sq) * search_co
        residual_sq = fresh_sq
    return sol_co, resid_co, search_co


def reference(populations, concentrations, potential, solid_mask, surface_sign):
    highest = lax.Precision.HIGHEST
    fluid_mask = 1.0 - solid_mask.astype(jnp.float32)
    efield = [(jnp.roll(potential, 1, axis_id) - jnp.roll(potential, -1, axis_id)) * 0.5 for axis_id in range(3)]
    fields = [populations[member] for member in range(19)]
    concentration = concentrations
    for time_step in range(STEPS):
        relaxed, velocity = collide_cells(fields, concentration, fluid_mask, efield)
        updated = []
        for member in range(19):
            offset = lattice_velocity[member]
            arrived = jnp.roll(relaxed[member], offset, axis=(0, 1, 2))
            source_open = jnp.roll(fluid_mask, offset, axis=(0, 1, 2))
            updated.append(jnp.where(fluid_mask > 0.5, jnp.where(source_open > 0.5, arrived, relaxed[opposite[member]]), fields[member]))
        concentration = ion_update(concentration, potential, velocity, fluid_mask)
        fields = updated
    target = fluid_mask * ion_charge(concentration) + surface_scale * surface_sign.astype(jnp.float32) * (1.0 - fluid_mask)
    solution = potential
    residual = target - (diag_coef * solution - neighbor_sum(solution[None])[0])
    search = residual
    for cycle_id in range(CYCLES):
        p_levels = [search]
        r_levels = [residual]
        current = jnp.stack([search, residual])
        previous = None
        for level_id in range(SSTEP):
            if level_id == SSTEP - 1:
                current = current[:1]
            following = next_level(neighbor_sum(current), None if level_id == 0 else previous[:current.shape[0]])
            previous = current
            current = following
            p_levels.append(current[0])
            if current.shape[0] > 1:
                r_levels.append(current[1])
        basis = jnp.stack(p_levels + r_levels)
        gram_matrix = jnp.einsum("aijk,bijk->ab", basis, basis, precision=highest)
        sol_co, resid_co, search_co = krylov_steps(gram_matrix)
        solution = solution + jnp.tensordot(sol_co, basis, axes=1, precision=highest)
        residual = jnp.tensordot(resid_co, basis, axes=1, precision=highest)
        search = jnp.tensordot(search_co, basis, axes=1, precision=highest)
    return jnp.stack(fields), concentration, solution
```

```python
import jax
import jax.numpy as jnp
from jax import lax
from jax.experimental import pallas as pl
from jax.experimental.pallas import tpu as pltpu
from jax.sharding import PartitionSpec as P

STEPS = 4
ITERS = 8

lattice_velocity = (
    (0, 0, 0),
    (0, 0, 1),
    (0, 0, -1),
    (0, 1, 0),
    (0, -1, 0),
    (1, 0, 0),
    (-1, 0, 0),
    (0, 1, 1),
    (0, -1, -1),
    (0, 1, -1),
    (0, -1, 1),
    (1, 0, 1),
    (-1, 0, -1),
    (1, 0, -1),
    (-1, 0, 1),
    (1, 1, 0),
    (-1, -1, 0),
    (1, -1, 0),
    (-1, 1, 0),
)
opposite = (0, 2, 1, 4, 3, 6, 5, 8, 7, 10, 9, 12, 11, 14, 13, 16, 15, 18, 17)
lattice_weight = (1.0 / 3.0,) + (1.0 / 18.0,) * 6 + (1.0 / 36.0,) * 12
relax_time = 1.25
force_scale = 0.05
valences = (1.0, -1.0, 2.0)
diffusivity = (0.05, 0.07, 0.03)
diag_coef = 6.0001
surface_scale = 2.0

FIELDS = 25
XT = 7
F_CONC, F_FLUID, F_POT, F_POT2 = 19, 22, 23, 24
SLABS = 9
TILE = (8, 128)


def lane_id():
    return lax.broadcasted_iota(jnp.int32, TILE, 1)


def row_id():
    return lax.broadcasted_iota(jnp.int32, TILE, 0)


def rl(v, amount):
    amount = amount % 128
    return v if amount == 0 else pltpu.roll(v, amount, 1)


def rs(v, amount):
    amount = amount % 8
    return v if amount == 0 else pltpu.roll(v, amount, 0)


def in_lanes(lane, start, width):
    return (lane >= start) & (lane < start + width)


def pack_kernel(pop, conc, pot, solid, x_left, x_right, y_down, y_up):
    lane, row = lane_id(), row_id()
    top = row < 4

    def tile(k, z):
        if k < F_CONC:
            return pop[k, z]
        if k < F_FLUID:
            return conc[k - F_CONC, z]
        if k == F_FLUID:
            return 1.0 - solid[z].astype(jnp.float32)
        return pot[z]

    for t in range(XT):
        left = right = jnp.zeros(TILE, jnp.float32)
        for q in range(4):
            k = 4 * t + q
            if k >= FIELDS:
                continue
            inner = 4 if k == F_POT2 else 0
            for z in range(8):
                v = tile(k, z)
                at = 16 * z + 4 * q
                here = in_lanes(lane, at, 4)
                left = jnp.where(here, rl(v, at - inner), left)
                right = jnp.where(here, rl(v, at - (124 - inner)), right)
        x_left[t] = left
        x_right[t] = right
    for k in range(FIELDS):
        for pair in range(4):
            a, b = tile(k, 2 * pair), tile(k, 2 * pair + 1)
            low = jnp.where(top, a, rs(b, 4))
            high = jnp.where(top, rs(a, 4), b)
            if k == F_POT2:
                low, high = high, low
            y_down[4 * k + pair] = low
            y_up[4 * k + pair] = high


def step_kernel(
    pop, conc, pot, solid, sign, up, down, from_right, from_left, corner_up, corner_down,
    pop_out, conc_out, edge_out,
    f, g, vel, cc, fluid, pt, mask, dpot, field,
):
    lane, row = lane_id(), row_id()
    top = row < 4
    slot = lane % 16
    first_row, last_row = row == 0, row == 7
    first_lane, last_lane = lane == 0, lane == 127

    def halves(k, z):
        u, d = up[4 * k + z // 2], down[4 * k + z // 2]
        if z % 2 == 0:
            return jnp.where(top, u, rs(d, 4))
        return jnp.where(top, rs(u, 4), d)

    def strip(k, tiles, low, high):
        q = k % 4
        out = jnp.where(slot < 4, rl(low, -4 * q), rl(high, 12 - 4 * q))
        for z in range(8):
            out = jnp.where(in_lanes(lane, 16 * z + 4, 4), rl(tiles[z], 16 * z + 4), out)
            out = jnp.where(in_lanes(lane, 16 * z + 8, 4), rl(tiles[z], 16 * z + 8 - 124), out)
        return out

    def load(k, own, put):
        t = k // 4
        a = [own(z) for z in range(8)]
        b = [halves(k, z) for z in range(8)]
        for z in range(8):
            put(2 * z, a[z])
            put(2 * z + 1, b[z])
        put(16, strip(k, a, from_left[t], from_right[t]))
        low = jnp.where(top, corner_up[XT + t], corner_down[XT + t])
        high = jnp.where(top, corner_up[t], corner_down[t])
        put(17, strip(k, b, low, high))

    def putter(ref, *index):
        def put(i, v):
            ref[(*index, i)] = v

        return put

    for k in range(19):
        load(k, lambda z, k=k: pop[k, z], putter(f, k))
    for k in range(3):
        load(F_CONC + k, lambda z, k=k: conc[k, z], putter(cc, 0, k))
    load(F_FLUID, lambda z: 1.0 - solid[z].astype(jnp.float32), putter(fluid))
    load(F_POT, lambda z: pot[z], putter(pt))

    def y_shift(a, b, cy):
        if cy == 0:
            return a, b
        edge = first_row if cy > 0 else last_row
        ra, rb = rs(a, cy), rs(b, cy)
        return jnp.where(edge, rb, ra), jnp.where(edge, ra, rb)

    def x_shift(v, side, z, cx):
        if cx > 0:
            return jnp.where(first_lane, rl(side, -(16 * z + 3)), rl(v, 1))
        return jnp.where(last_lane, rl(side, 127 - (16 * z + 12)), rl(v, -1))

    def shifted(get, offset):
        cz, cy, cx = offset
        side = y_shift(get(16), get(17), cy)
        out = []
        for z in range(8):
            source = (z - cz) % 8
            v = y_shift(get(2 * source), get(2 * source + 1), cy)
            if cx:
                v = tuple(x_shift(v[h], side[h], source, cx) for h in range(2))
            out.append(v)
        out.append(tuple(rl(side[h], 16 * cz + cx) for h in range(2)))
        return out

    for i in range(1, 19):
        moved = shifted(lambda s: fluid[s], lattice_velocity[i])
        for s in range(SLABS):
            for h in range(2):
                mask[i - 1, 2 * s + h] = moved[s][h] * fluid[2 * s + h]

    far = [halves(F_POT2, z) for z in range(8)]
    t2, q2 = F_POT2 // 4, F_POT2 % 4
    tp = F_POT // 4
    far_low = jnp.where(top, rs(corner_up[XT + tp], 4), rs(corner_down[XT + tp], 4))
    far_high = jnp.where(top, rs(corner_up[tp], 4), rs(corner_down[tp], 4))
    far.append(strip(F_POT, far, far_low, far_high))
    edge_low = (from_left[t2], jnp.where(top, corner_up[XT + t2], corner_down[XT + t2]))
    edge_high = (from_right[t2], jnp.where(top, corner_up[t2], corner_down[t2]))
    for axis in range(3):
        plus = tuple(1 if d == axis else 0 for d in range(3))
        minus = tuple(-p for p in plus)
        below = shifted(lambda s: pt[s], plus)
        above = shifted(lambda s: pt[s], minus)
        for s in range(SLABS):
            for h in range(2):
                lo, hi = below[s][h], above[s][h]
                if axis == 1 and h == 1:
                    lo = jnp.where(row == 4, rs(far[s], -3), lo)
                    hi = jnp.where(row == 3, rs(far[s], 3), hi)
                if axis == 2 and s == 8:
                    lo = jnp.where(slot == 0, rl(edge_low[h], -4 * q2 - 3), lo)
                    hi = jnp.where(slot == 15, rl(edge_high[h], 15 - 4 * q2), hi)
                here = pt[2 * s + h]
                dpot[2 * axis, 2 * s + h] = here - lo
                dpot[2 * axis + 1, 2 * s + h] = hi - here
                field[axis, 2 * s + h] = (0.5 * force_scale) * (lo - hi)

    pairs = [(i, i + 1) for i in range(1, 19, 2)]

    def collide(s, now):
        v = [f[i, s] for i in range(19)]
        total = {}
        delta = {}
        for a, b in pairs:
            total[a] = v[a] + v[b]
            delta[a] = v[a] - v[b]
        density = (
            v[0]
            + ((total[1] + total[3]) + (total[5] + total[7]))
            + ((total[9] + total[11]) + (total[13] + total[15]) + total[17])
        )
        momentum = (
            (delta[5] + delta[11]) + (delta[13] + delta[15]) + delta[17],
            (delta[3] + delta[7]) + (delta[9] + delta[15]) - delta[17],
            (delta[1] + delta[7]) - (delta[9] - delta[11]) - delta[13],
        )
        open_cell = fluid[s]
        charge = open_cell * (
            valences[0] * cc[now, 0, s] + valences[1] * cc[now, 1, s] + valences[2] * cc[now, 2, s]
        )
        force = [charge * field[d, s] for d in range(3)]
        inverse = 1.0 / density
        u = [(momentum[d] + 0.5 * force[d]) * inverse for d in range(3)]
        for d in range(3):
            vel[d, s] = u[d]
        speed = u[0] * u[0] + u[1] * u[1] + u[2] * u[2]
        work = u[0] * force[0] + u[1] * force[1] + u[2] * force[2]
        flow = [density * u[d] for d in range(3)]
        keep = 1.0 - 1.0 / relax_time
        gain = 1.0 / relax_time
        push = 1.0 - 0.5 / relax_time
        base = gain * density - (1.5 * gain) * (density * speed) - (3.0 * push) * work
        odd = [(3.0 * gain) * flow[d] + (3.0 * push) * force[d] for d in range(3)]
        even = [(4.5 * gain) * flow[d] + (9.0 * push) * force[d] for d in range(3)]
        is_open = open_cell > 0.5
        g[0, s] = jnp.where(is_open, keep * v[0] + lattice_weight[0] * base, v[0])

        def along(c, vector):
            running = None
            for d in range(3):
                if c[d] != 0:
                    if running is None:
                        running = vector[d] if c[d] > 0 else -vector[d]
                    else:
                        running = running + vector[d] if c[d] > 0 else running - vector[d]
            return running

        for a, b in pairs:
            c, w = lattice_velocity[a], lattice_weight[a]
            middle = base + along(c, u) * along(c, even)
            side = along(c, odd)
            g[a, s] = jnp.where(is_open, keep * v[a] + w * (middle + side), v[b])
            g[b, s] = jnp.where(is_open, keep * v[b] + w * (middle - side), v[a])

    def one_step(step, carry):
        now = lax.rem(step, 2)
        after = 1 - now

        def both(s, c):
            collide(2 * s, now)
            collide(2 * s + 1, now)
            return c

        lax.fori_loop(0, SLABS, both, 0)
        for s in range(2 * SLABS):
            f[0, s] = g[0, s]
        for i in range(1, 19):
            moved = shifted(lambda s, i=i: g[i, s], lattice_velocity[i])
            for s in range(SLABS):
                for h in range(2):
                    n = 2 * s + h
                    f[i, n] = jnp.where(mask[i - 1, n] > 0.5, moved[s][h], g[opposite[i], n])
        for k in range(3):
            for s in range(2 * SLABS):
                cc[after, k, s] = cc[now, k, s]
        for axis in range(3):
            plus = tuple(1 if d == axis else 0 for d in range(3))
            minus = tuple(-p for p in plus)
            lower = 2 * (2 - axis)
            v_low = shifted(lambda s: vel[axis, s], plus)
            v_high = shifted(lambda s: vel[axis, s], minus)
            for k in range(3):
                c_low = shifted(lambda s: cc[now, k, s], plus)
                c_high = shifted(lambda s: cc[now, k, s], minus)
                rate = diffusivity[k]
                drift = 0.5 * rate * valences[k]
                for s in range(SLABS):
                    for h in range(2):
                        n = 2 * s + h
                        here, v_here = cc[now, k, n], vel[axis, n]
                        lo, hi = c_low[s][h], c_high[s][h]
                        carry_low = 0.25 * (v_low[s][h] + v_here) - drift * dpot[2 * axis, n]
                        carry_high = 0.25 * (v_here + v_high[s][h]) - drift * dpot[2 * axis + 1, n]
                        flux_low = mask[lower, n] * (rate * (lo - here) + (lo + here) * carry_low)
                        flux_high = mask[lower + 1, n] * (rate * (here - hi) + (here + hi) * carry_high)
                        cc[after, k, n] = cc[after, k, n] - (flux_high - flux_low)
        return carry

    lax.fori_loop(0, STEPS, one_step, 0)

    last = STEPS % 2
    edge = jnp.zeros(TILE, jnp.float32)
    for z in range(8):
        n = 2 * z
        for i in range(19):
            pop_out[i, z] = f[i, n]
        c = [cc[last, k, n] for k in range(3)]
        for k in range(3):
            conc_out[k, z] = c[k]
        open_cell = fluid[n]
        target = open_cell * (
            valences[0] * c[0] + valences[1] * c[1] + valences[2] * c[2]
        ) + surface_scale * sign[z].astype(jnp.float32) * (1.0 - open_cell)
        spread = (
            (dpot[1, n] - dpot[0, n]) + (dpot[3, n] - dpot[2, n]) + (dpot[5, n] - dpot[4, n])
        )
        residual = target - ((diag_coef - 6.0) * pt[n] - spread)
        edge_out[z] = residual
        edge = jnp.where(in_lanes(lane, 16 * z, 8), rl(residual, 16 * z - 120), edge)
        edge = jnp.where(in_lanes(lane, 16 * z + 8, 8), rl(residual, 16 * z + 8), edge)
    edge_out[8] = edge


def levels_kernel(own, left, right, up, down, level_out, moment_out, lv):
    lane, row = lane_id(), row_id()
    slot = lane % 16
    first_row, last_row = row == 0, row == 7
    first_lane, last_lane = lane == 0, lane == 127
    sources = (
        (own, left[0], right[0]),
        (up, up[9], up[10]),
        (down, down[9], down[10]),
    )
    for r, (main, low, high) in enumerate(sources):
        for s in range(8):
            lv[0, r, s] = main[s]
        lv[0, r, 8] = jnp.where(slot < 8, low, main[8])
        lv[0, r, 9] = jnp.where(slot < 8, main[8], high)

    def around(j, r, s, low, high):
        v = lv[j, r, s]
        above, below = lv[j, (r + 1) % 3, s], lv[j, (r + 2) % 3, s]
        vertical = jnp.where(last_row, rs(above, -1), rs(v, -1)) + jnp.where(
            first_row, rs(below, 1), rs(v, 1)
        )
        if s < 8:
            across = jnp.where(first_lane, rl(low, -(16 * s + 7)), rl(v, 1)) + jnp.where(
                last_lane, rl(high, 127 - (16 * s + 8)), rl(v, -1)
            )
            return (lv[j, r, (s + 1) % 8] + lv[j, r, (s - 1) % 8]) + vertical + across
        return (rl(v, 16) + rl(v, -16)) + vertical + (rl(v, 1) + rl(v, -1))

    for j in range(ITERS):
        done = j == ITERS - 1
        squares = products = jnp.zeros(TILE, jnp.float32)
        for r in range(1 if done else 3):
            low, high = lv[j, r, 8], lv[j, r, 9]
            for s in range(8 if done else 10):
                total = around(j, r, s, low, high)
                if j == 0:
                    fresh = -total / 6.0
                else:
                    fresh = total * (-1.0 / 3.0) - lv[j - 1, r, s]
                if not done:
                    lv[j + 1, r, s] = fresh
                if r == 0 and s < 8:
                    here = lv[j, 0, s]
                    level_out[j, s] = here
                    squares = squares + here * here
                    products = products + here * fresh
        moment_out[j : j + 1, :] = jnp.sum(squares, axis=0, keepdims=True)
        moment_out[8 + j : 9 + j, :] = jnp.sum(products, axis=0, keepdims=True)


def combine_kernel(moments, levels, pot, out):
    sums = jnp.sum(moments[...], axis=1, keepdims=True)

    def entry(i):
        return jnp.broadcast_to(sums[i : i + 1, :], TILE)

    moment = [None] * 16
    moment[0], moment[1] = entry(0), entry(8)
    for k in range(1, ITERS):
        moment[2 * k] = 2.0 * entry(k) - moment[0]
        moment[2 * k + 1] = 2.0 * entry(8 + k) - moment[1]
    gram = {}
    for i in range(ITERS + 1):
        for j in range(i, ITERS + 1):
            if i + j < 16:
                gram[i, j] = gram[j, i] = 0.5 * (moment[i + j] + moment[j - i])

    def inner(a, b):
        running = None
        for i, x in enumerate(a):
            row = None
            for j, y in enumerate(b):
                term = gram[i, j] * y
                row = term if row is None else row + term
            row = x * row
            running = row if running is None else running + row
        return running

    one, zero = jnp.ones(TILE, jnp.float32), jnp.zeros(TILE, jnp.float32)
    search, rest, found = [one], [one], []
    left = moment[0]
    for k in range(ITERS):
        image = [zero] * (k + 2)
        for j in range(k + 1):
            image[j] = image[j] + diag_coef * search[j]
            if j == 0:
                image[1] = image[1] + 6.0 * search[0]
            else:
                image[j + 1] = image[j + 1] + 3.0 * search[j]
                image[j - 1] = image[j - 1] + 3.0 * search[j]
        length = left / inner(search, image)
        found = [
            (found[j] if j < len(found) else zero) + length * search[j] for j in range(k + 1)
        ]
        if k == ITERS - 1:
            break
        rest = [(rest[j] if j < k + 1 else zero) - length * image[j] for j in range(k + 2)]
        fresh = inner(rest, rest)
        ratio = fresh / left
        search = [rest[j] + (ratio * search[j] if j < k + 1 else zero) for j in range(k + 2)]
        left = fresh
    for z in range(8):
        running = found[0] * levels[0, z]
        for j in range(1, ITERS):
            running = running + found[j] * levels[j, z]
        out[z] = pot[z] + running


def in_vmem(count):
    return [pl.BlockSpec(memory_space=pltpu.VMEM)] * count


def f32(*shape):
    return jax.ShapeDtypeStruct(shape, jnp.float32)


def call(kernel, name, outs, scratch, *args):
    return pl.pallas_call(
        kernel,
        name=name,
        out_shape=outs,
        in_specs=in_vmem(len(args)),
        out_specs=in_vmem(len(outs)),
        scratch_shapes=[pltpu.VMEM(shape, jnp.float32) for shape in scratch],
        compiler_params=pltpu.CompilerParams(vmem_limit_bytes=48 << 20),
    )(*args)


def send(block, axis, step):
    count = lax.axis_size(axis)
    return lax.ppermute(block, axis, [(i, (i + step) % count) for i in range(count)])


def total_over(block, axis):
    count = lax.axis_size(axis)
    step = 1
    while step < count:
        if step * 4 <= count:
            parts = [
                lax.ppermute(block, axis, [(i, i ^ (k * step)) for i in range(count)])
                for k in (1, 2, 3)
            ]
            block = (block + parts[0]) + (parts[1] + parts[2])
            step *= 4
        else:
            block = block + lax.ppermute(block, axis, [(i, i ^ step) for i in range(count)])
            step *= 2
    return block


def local(populations, concentrations, potential, solid_mask, surface_sign):
    x_left, x_right, y_down, y_up = call(
        pack_kernel,
        "pack",
        (f32(XT, 8, 128), f32(XT, 8, 128), f32(4 * FIELDS, 8, 128), f32(4 * FIELDS, 8, 128)),
        [],
        populations,
        concentrations,
        potential,
        solid_mask,
    )
    up = send(y_down, "gy", -1)
    down = send(y_up, "gy", 1)
    from_right = send(x_left, "gx", -1)
    from_left = send(x_right, "gx", 1)
    corner = jnp.concatenate([from_right, from_left])
    corner_up = send(corner, "gy", -1)
    corner_down = send(corner, "gy", 1)
    n = 2 * SLABS
    pop_new, conc_new, edge = call(
        step_kernel,
        "steps",
        (f32(19, 8, 8, 128), f32(3, 8, 8, 128), f32(9, 8, 128)),
        [
            (19, n, 8, 128),
            (19, n, 8, 128),
            (3, n, 8, 128),
            (2, 3, n, 8, 128),
            (n, 8, 128),
            (n, 8, 128),
            (18, n, 8, 128),
            (6, n, 8, 128),
            (3, n, 8, 128),
        ],
        populations,
        concentrations,
        potential,
        solid_mask,
        surface_sign,
        up,
        down,
        from_right,
        from_left,
        corner_up,
        corner_down,
    )
    strip = edge[8:]
    left = send(strip, "gx", 1)
    right = send(strip, "gx", -1)
    wide = jnp.concatenate([edge, left, right])
    above = send(wide, "gy", -1)
    below = send(wide, "gy", 1)
    levels, moments = call(
        levels_kernel,
        "levels",
        (f32(ITERS, 8, 8, 128), f32(16, 128)),
        [(ITERS, 3, 10, 8, 128)],
        edge,
        left,
        right,
        above,
        below,
    )
    moments = total_over(total_over(moments, "gx"), "gy")
    (pot_new,) = call(combine_kernel, "combine", (f32(8, 8, 128),), [], moments, levels, potential)
    return (pop_new, conc_new, pot_new)


def solution(mesh):
    placed = (
        P(None, None, "gy", "gx"),
        P(None, None, "gy", "gx"),
        P(None, "gy", "gx"),
        P(None, "gy", "gx"),
        P(None, "gy", "gx"),
    )
    return jax.shard_map(
        local,
        mesh=mesh,
        in_specs=placed,
        out_specs=(P(None, None, "gy", "gx"), P(None, None, "gy", "gx"), P(None, "gy", "gx")),
        check_vma=False,
    )
```

```python
import jax
import jax.numpy as jnp
from jax import lax
from jax.experimental import pallas as pl
from jax.experimental.pallas import tpu as pltpu
from jax.sharding import PartitionSpec as P

STEPS = 4
ITERS = 8

lattice_velocity = (
    (0, 0, 0),
    (0, 0, 1),
    (0, 0, -1),
    (0, 1, 0),
    (0, -1, 0),
    (1, 0, 0),
    (-1, 0, 0),
    (0, 1, 1),
    (0, -1, -1),
    (0, 1, -1),
    (0, -1, 1),
    (1, 0, 1),
    (-1, 0, -1),
    (1, 0, -1),
    (-1, 0, 1),
    (1, 1, 0),
    (-1, -1, 0),
    (1, -1, 0),
    (-1, 1, 0),
)
opposite = (0, 2, 1, 4, 3, 6, 5, 8, 7, 10, 9, 12, 11, 14, 13, 16, 15, 18, 17)
lattice_weight = (1.0 / 3.0,) + (1.0 / 18.0,) * 6 + (1.0 / 36.0,) * 12
relax_time = 1.25
force_scale = 0.05
valences = (1.0, -1.0, 2.0)
diffusivity = (0.05, 0.07, 0.03)
diag_coef = 6.0001
surface_scale = 2.0

FIELDS = 25
XT = 7
F_CONC, F_FLUID, F_POT, F_POT2 = 19, 22, 23, 24
SLABS = 9
TILE = (8, 128)


def lane_id():
    return lax.broadcasted_iota(jnp.int32, TILE, 1)


def row_id():
    return lax.broadcasted_iota(jnp.int32, TILE, 0)


def rl(v, amount):
    amount = amount % 128
    return v if amount == 0 else pltpu.roll(v, amount, 1)


def rs(v, amount):
    amount = amount % 8
    return v if amount == 0 else pltpu.roll(v, amount, 0)


def in_lanes(lane, start, width):
    return (lane >= start) & (lane < start + width)


def pack_kernel(*refs):
    sources, copies = refs[:5], refs[5:10]
    x_left, x_right, y_down, y_up, sems = refs[10:]
    moves = [
        pltpu.make_async_copy(sources[i], copies[i], sems.at[i]) for i in (0, 1, 2, 3, 4)
    ]
    for move in moves:
        move.start()
    pop, conc, pot, solid = copies[:4]
    lane, row = lane_id(), row_id()
    top = row < 4
    for move in moves:
        move.wait()

    def tile(k, z):
        if k < F_CONC:
            return pop[k, z]
        if k < F_FLUID:
            return conc[k - F_CONC, z]
        if k == F_FLUID:
            return 1.0 - solid[z].astype(jnp.float32)
        return pot[z]

    for t in range(XT):
        left = right = jnp.zeros(TILE, jnp.float32)
        for q in range(4):
            k = 4 * t + q
            if k >= FIELDS:
                continue
            inner = 4 if k == F_POT2 else 0
            for z in range(8):
                v = tile(k, z)
                at = 16 * z + 4 * q
                here = in_lanes(lane, at, 4)
                left = jnp.where(here, rl(v, at - inner), left)
                right = jnp.where(here, rl(v, at - (124 - inner)), right)
        x_left[t] = left
        x_right[t] = right
    for k in range(FIELDS):
        for pair in range(4):
            a, b = tile(k, 2 * pair), tile(k, 2 * pair + 1)
            low = jnp.where(top, a, rs(b, 4))
            high = jnp.where(top, rs(a, 4), b)
            if k == F_POT2:
                low, high = high, low
            y_down[4 * k + pair] = low
            y_up[4 * k + pair] = high


def y_shift(a, b, cy, halves=(0, 1)):
    if cy == 0:
        return a, b
    edge = row_id() == (0 if cy > 0 else 7)
    ra, rb = rs(a, cy), rs(b, cy)
    return tuple(jnp.where(edge, rb, ra) if h == 0 else jnp.where(edge, ra, rb) for h in halves)


def x_shift(v, side, z, cx):
    if cx > 0:
        return jnp.where(lane_id() == 0, rl(side, -(16 * z + 3)), rl(v, 1))
    return jnp.where(lane_id() == 127, rl(side, 127 - (16 * z + 12)), rl(v, -1))


def shifted(get, offset, own=False):
    cz, cy, cx = offset
    halves = (0,) if own else (0, 1)
    side = y_shift(get(16), get(17), cy, halves) if cx or not own else None
    out = []
    for z in range(8):
        source = (z - cz) % 8
        v = y_shift(get(2 * source), get(2 * source + 1), cy, halves)
        if cx:
            v = tuple(x_shift(v[h], side[h], source, cx) for h in halves)
        out.append(v)
    if not own:
        out.append(tuple(rl(side[h], 16 * cz + cx) for h in halves))
    return out


def step_kernel(
    pop, conc, pot, solid, sign, up, down, from_right, from_left, corner_up, corner_down,
    g, mask, conc_out, edge_out,
    f, vel, cc, fluid, pt, dpot, field, speed_up, flux,
):
    lane, row = lane_id(), row_id()
    top = row < 4
    slot = lane % 16

    def halves(k, z):
        u, d = up[4 * k + z // 2], down[4 * k + z // 2]
        if z % 2 == 0:
            return jnp.where(top, u, rs(d, 4))
        return jnp.where(top, rs(u, 4), d)

    def strip(k, tiles, low, high):
        q = k % 4
        out = jnp.where(slot < 4, rl(low, -4 * q), rl(high, 12 - 4 * q))
        for z in range(8):
            out = jnp.where(in_lanes(lane, 16 * z + 4, 4), rl(tiles[z], 16 * z + 4), out)
            out = jnp.where(in_lanes(lane, 16 * z + 8, 4), rl(tiles[z], 16 * z + 8 - 124), out)
        return out

    def load(k, own, put):
        t = k // 4
        a = [own(z) for z in range(8)]
        b = [halves(k, z) for z in range(8)]
        for z in range(8):
            put(2 * z, a[z])
            put(2 * z + 1, b[z])
        put(16, strip(k, a, from_left[t], from_right[t]))
        low = jnp.where(top, corner_up[XT + t], corner_down[XT + t])
        high = jnp.where(top, corner_up[t], corner_down[t])
        put(17, strip(k, b, low, high))

    def putter(ref, *index):
        def put(i, v):
            ref[(*index, i)] = v

        return put

    for k in range(19):
        load(k, lambda z, k=k: pop[k, z], putter(f, k))
    for k in range(3):
        load(F_CONC + k, lambda z, k=k: conc[k, z], putter(cc, 0, k))
    load(F_FLUID, lambda z: 1.0 - solid[z].astype(jnp.float32), putter(fluid))
    load(F_POT, lambda z: pot[z], putter(pt))

    for i in range(1, 19):
        moved = shifted(lambda s: fluid[s], lattice_velocity[i])
        for s in range(SLABS):
            for h in range(2):
                mask[i - 1, 2 * s + h] = moved[s][h] * fluid[2 * s + h]

    far = [halves(F_POT2, z) for z in range(8)]
    t2, q2 = F_POT2 // 4, F_POT2 % 4
    tp = F_POT // 4
    far_low = jnp.where(top, rs(corner_up[XT + tp], 4), rs(corner_down[XT + tp], 4))
    far_high = jnp.where(top, rs(corner_up[tp], 4), rs(corner_down[tp], 4))
    far.append(strip(F_POT, far, far_low, far_high))
    edge_low = (from_left[t2], jnp.where(top, corner_up[XT + t2], corner_down[XT + t2]))
    edge_high = (from_right[t2], jnp.where(top, corner_up[t2], corner_down[t2]))
    for axis in range(3):
        plus = tuple(1 if d == axis else 0 for d in range(3))
        minus = tuple(-p for p in plus)
        below = shifted(lambda s: pt[s], plus)
        above = shifted(lambda s: pt[s], minus)
        for s in range(SLABS):
            for h in range(2):
                lo, hi = below[s][h], above[s][h]
                if axis == 1 and h == 1:
                    lo = jnp.where(row == 4, rs(far[s], -3), lo)
                    hi = jnp.where(row == 3, rs(far[s], 3), hi)
                if axis == 2 and s == 8:
                    lo = jnp.where(slot == 0, rl(edge_low[h], -4 * q2 - 3), lo)
                    hi = jnp.where(slot == 15, rl(edge_high[h], 15 - 4 * q2), hi)
                    for z in range(8):
                        hi = jnp.where(lane == 16 * z + 7, rl(pt[2 * z + h], 16 * z + 3), hi)
                here = pt[2 * s + h]
                dpot[2 * axis, 2 * s + h] = here - lo
                dpot[2 * axis + 1, 2 * s + h] = hi - here
                field[axis, 2 * s + h] = (0.5 * force_scale) * (lo - hi)

    pairs = [(i, i + 1) for i in range(1, 19, 2)]

    def collide(s, now):
        v = [f[i, s] for i in range(19)]
        total = {}
        delta = {}
        for a, b in pairs:
            total[a] = v[a] + v[b]
            delta[a] = v[a] - v[b]
        density = (
            v[0]
            + ((total[1] + total[3]) + (total[5] + total[7]))
            + ((total[9] + total[11]) + (total[13] + total[15]) + total[17])
        )
        momentum = (
            (delta[5] + delta[11]) + (delta[13] + delta[15]) + delta[17],
            (delta[3] + delta[7]) + (delta[9] + delta[15]) - delta[17],
            (delta[1] + delta[7]) - (delta[9] - delta[11]) - delta[13],
        )
        open_cell = fluid[s]
        charge = open_cell * (
            valences[0] * cc[now, 0, s] + valences[1] * cc[now, 1, s] + valences[2] * cc[now, 2, s]
        )
        force = [charge * field[d, s] for d in range(3)]
        inverse = 1.0 / density
        u = [(momentum[d] + 0.5 * force[d]) * inverse for d in range(3)]
        for d in range(3):
            vel[d, s] = u[d]
        speed = u[0] * u[0] + u[1] * u[1] + u[2] * u[2]
        work = u[0] * force[0] + u[1] * force[1] + u[2] * force[2]
        flow = [density * u[d] for d in range(3)]
        keep = 1.0 - 1.0 / relax_time
        gain = 1.0 / relax_time
        push = 1.0 - 0.5 / relax_time
        base = gain * density - (1.5 * gain) * (density * speed) - (3.0 * push) * work
        odd = [(3.0 * gain) * flow[d] + (3.0 * push) * force[d] for d in range(3)]
        even = [(4.5 * gain) * flow[d] + (9.0 * push) * force[d] for d in range(3)]
        is_open = open_cell > 0.5
        g[0, s] = jnp.where(is_open, keep * v[0] + lattice_weight[0] * base, v[0])

        def along(c, vector):
            running = None
            for d in range(3):
                if c[d] != 0:
                    if running is None:
                        running = vector[d] if c[d] > 0 else -vector[d]
                    else:
                        running = running + vector[d] if c[d] > 0 else running - vector[d]
            return running

        for a, b in pairs:
            c, w = lattice_velocity[a], lattice_weight[a]
            middle = base + along(c, u) * along(c, even)
            side = along(c, odd)
            g[a, s] = jnp.where(is_open, keep * v[a] + w * (middle + side), v[b])
            g[b, s] = jnp.where(is_open, keep * v[b] + w * (middle - side), v[a])

    def collide_all(now):
        def both(s, c):
            collide(2 * s, now)
            collide(2 * s + 1, now)
            return c

        lax.fori_loop(0, SLABS, both, 0)

    def stream():
        for s in range(2 * SLABS):
            f[0, s] = g[0, s]
        for i in range(1, 19):
            moved = shifted(lambda s, i=i: g[i, s], lattice_velocity[i])
            for s in range(SLABS):
                for h in range(2):
                    n = 2 * s + h
                    f[i, n] = jnp.where(mask[i - 1, n] > 0.5, moved[s][h], g[opposite[i], n])

    def ions(now, after, own=False):
        for axis in range(3):
            plus = tuple(1 if d == axis else 0 for d in range(3))
            minus = tuple(-p for p in plus)
            upper = 2 * (2 - axis) + 1
            v_high = shifted(lambda s: vel[axis, s], minus)
            for s in range(SLABS):
                for h in range(2):
                    n = 2 * s + h
                    speed_up[n] = 0.25 * (vel[axis, n] + v_high[s][h])
            for k in range(3):
                c_high = shifted(lambda s: cc[now, k, s], minus)
                rate = diffusivity[k]
                drift = 0.5 * rate * valences[k]
                for s in range(SLABS):
                    for h in range(2):
                        n = 2 * s + h
                        here, hi = cc[now, k, n], c_high[s][h]
                        pull = speed_up[n] - drift * dpot[2 * axis + 1, n]
                        flux[k, n] = mask[upper, n] * (rate * (here - hi) + (here + hi) * pull)
                low = shifted(lambda s: flux[k, s], plus, own)
                for s in range(8 if own else SLABS):
                    for h in range(1 if own else 2):
                        n = 2 * s + h
                        before = cc[now if axis == 0 else after, k, n]
                        cc[after, k, n] = before - (flux[k, n] - low[s][h])

    def one_step(step, carry):
        now = lax.rem(step, 2)
        collide_all(now)
        stream()
        ions(now, 1 - now)
        return carry

    lax.fori_loop(0, STEPS - 1, one_step, 0)
    final = (STEPS - 1) % 2
    collide_all(final)
    ions(final, 1 - final, own=True)

    last = STEPS % 2
    edge = jnp.zeros(TILE, jnp.float32)
    for z in range(8):
        n = 2 * z
        c = [cc[last, k, n] for k in range(3)]
        for k in range(3):
            conc_out[k, z] = c[k]
        open_cell = fluid[n]
        target = open_cell * (
            valences[0] * c[0] + valences[1] * c[1] + valences[2] * c[2]
        ) + surface_scale * sign[z].astype(jnp.float32) * (1.0 - open_cell)
        spread = (
            (dpot[1, n] - dpot[0, n]) + (dpot[3, n] - dpot[2, n]) + (dpot[5, n] - dpot[4, n])
        )
        residual = target - ((diag_coef - 6.0) * pt[n] - spread)
        edge_out[z] = residual
        edge = jnp.where(in_lanes(lane, 16 * z, 8), rl(residual, 16 * z - 120), edge)
        edge = jnp.where(in_lanes(lane, 16 * z + 8, 8), rl(residual, 16 * z + 8), edge)
    edge_out[8] = edge


def finish_kernel(g, mask, pop_out):
    for z in range(8):
        pop_out[0, z] = g[0, 2 * z]
    for i in range(1, 19):
        moved = shifted(lambda s, i=i: g[i, s], lattice_velocity[i], own=True)
        for z in range(8):
            pop_out[i, z] = jnp.where(mask[i - 1, 2 * z] > 0.5, moved[z][0], g[opposite[i], 2 * z])


def levels_kernel(own, left, right, up, down, level_out, row_out, lv, part):
    lane, row = lane_id(), row_id()
    slot = lane % 16
    first_row, last_row = row == 0, row == 7
    first_lane, last_lane = lane == 0, lane == 127
    sources = (
        (own, left[0], right[0]),
        (up, up[9], up[10]),
        (down, down[9], down[10]),
    )
    for r, (main, low, high) in enumerate(sources):
        for s in range(8):
            lv[0, r, s] = main[s]
        lv[0, r, 8] = jnp.where(slot < 8, low, main[8])
        lv[0, r, 9] = jnp.where(slot < 8, main[8], high)

    def around(j, r, s, low, high):
        v = lv[j, r, s]
        above, below = lv[j, (r + 1) % 3, s], lv[j, (r + 2) % 3, s]
        vertical = jnp.where(last_row, rs(above, -1), rs(v, -1)) + jnp.where(
            first_row, rs(below, 1), rs(v, 1)
        )
        if s < 8:
            across = jnp.where(first_lane, rl(low, -(16 * s + 7)), rl(v, 1)) + jnp.where(
                last_lane, rl(high, 127 - (16 * s + 8)), rl(v, -1)
            )
            return (lv[j, r, (s + 1) % 8] + lv[j, r, (s - 1) % 8]) + vertical + across
        return (rl(v, 16) + rl(v, -16)) + vertical + (rl(v, 1) + rl(v, -1))

    for j in range(ITERS):
        done = j == ITERS - 1
        squares = products = jnp.zeros(TILE, jnp.float32)
        for r in range(1 if done else 3):
            low, high = lv[j, r, 8], lv[j, r, 9]
            for s in range(8 if done else 10):
                total = around(j, r, s, low, high)
                if j == 0:
                    fresh = -total / 6.0
                else:
                    fresh = total * (-1.0 / 3.0) - lv[j - 1, r, s]
                if not done:
                    lv[j + 1, r, s] = fresh
                if r == 0 and s < 8:
                    here = lv[j, 0, s]
                    level_out[j, s] = here
                    squares = squares + here * here
                    products = products + here * fresh
        part[j : j + 1, :] = jnp.sum(squares, axis=0, keepdims=True)
        part[8 + j : 9 + j, :] = jnp.sum(products, axis=0, keepdims=True)
    sums = jnp.sum(part[...], axis=1, keepdims=True)
    diagonal = lax.broadcasted_iota(jnp.int32, (16, 128), 0) == lax.broadcasted_iota(
        jnp.int32, (16, 128), 1
    )
    one_row = jnp.sum(jnp.where(diagonal, sums, 0.0), axis=0, keepdims=True)
    row_out[...] = jnp.broadcast_to(one_row, row_out.shape)


def combine_kernel(rows, levels, pot, out):
    total = jnp.broadcast_to(jnp.sum(rows[...], axis=0, keepdims=True), (16, 128))
    diagonal = lax.broadcasted_iota(jnp.int32, (16, 128), 0) == lax.broadcasted_iota(
        jnp.int32, (16, 128), 1
    )
    sums = jnp.sum(jnp.where(diagonal, total, 0.0), axis=1, keepdims=True)

    def entry(i):
        return jnp.broadcast_to(sums[i : i + 1, :], TILE)

    moment = [None] * 16
    moment[0], moment[1] = entry(0), entry(8)
    for k in range(1, ITERS):
        moment[2 * k] = 2.0 * entry(k) - moment[0]
        moment[2 * k + 1] = 2.0 * entry(8 + k) - moment[1]
    gram = {}
    for i in range(ITERS + 1):
        for j in range(i, ITERS + 1):
            if i + j < 16:
                gram[i, j] = gram[j, i] = 0.5 * (moment[i + j] + moment[j - i])

    def inner(a, b):
        running = None
        for i, x in enumerate(a):
            row = None
            for j, y in enumerate(b):
                term = gram[i, j] * y
                row = term if row is None else row + term
            row = x * row
            running = row if running is None else running + row
        return running

    one, zero = jnp.ones(TILE, jnp.float32), jnp.zeros(TILE, jnp.float32)
    search, rest, found = [one], [one], []
    left = moment[0]
    for k in range(ITERS):
        image = [zero] * (k + 2)
        for j in range(k + 1):
            image[j] = image[j] + diag_coef * search[j]
            if j == 0:
                image[1] = image[1] + 6.0 * search[0]
            else:
                image[j + 1] = image[j + 1] + 3.0 * search[j]
                image[j - 1] = image[j - 1] + 3.0 * search[j]
        length = left / inner(search, image)
        found = [
            (found[j] if j < len(found) else zero) + length * search[j] for j in range(k + 1)
        ]
        if k == ITERS - 1:
            break
        rest = [(rest[j] if j < k + 1 else zero) - length * image[j] for j in range(k + 2)]
        fresh = inner(rest, rest)
        ratio = fresh / left
        search = [rest[j] + (ratio * search[j] if j < k + 1 else zero) for j in range(k + 2)]
        left = fresh
    for z in range(8):
        running = found[0] * levels[0, z]
        for j in range(1, ITERS):
            running = running + found[j] * levels[j, z]
        out[z] = pot[z] + running


def in_vmem(count):
    return [pl.BlockSpec(memory_space=pltpu.VMEM)] * count


def f32(*shape):
    return jax.ShapeDtypeStruct(shape, jnp.float32)


def call(kernel, name, outs, scratch, *args, in_specs=None):
    return pl.pallas_call(
        kernel,
        name=name,
        out_shape=outs,
        in_specs=in_specs or in_vmem(len(args)),
        out_specs=in_vmem(len(outs)),
        scratch_shapes=[
            pltpu.VMEM(shape, jnp.float32) if isinstance(shape, tuple) else shape
            for shape in scratch
        ],
        compiler_params=pltpu.CompilerParams(vmem_limit_bytes=48 << 20),
    )(*args)


def send(block, axis, step):
    count = lax.axis_size(axis)
    return lax.ppermute(block, axis, [(i, (i + step) % count) for i in range(count)])


def local(populations, concentrations, potential, solid_mask, surface_sign):
    inputs = (populations, concentrations, potential, solid_mask, surface_sign)
    packed = call(
        pack_kernel,
        "pack",
        tuple(jax.ShapeDtypeStruct(a.shape, a.dtype) for a in inputs)
        + (f32(XT, 8, 128), f32(XT, 8, 128), f32(4 * FIELDS, 8, 128), f32(4 * FIELDS, 8, 128)),
        [pltpu.SemaphoreType.DMA((5,))],
        *inputs,
        in_specs=[pl.BlockSpec(memory_space=pltpu.HBM)] * 5,
    )
    kept, (x_left, x_right, y_down, y_up) = packed[:5], packed[5:]
    up = send(y_down, "gy", -1)
    down = send(y_up, "gy", 1)
    from_right = send(x_left, "gx", -1)
    from_left = send(x_right, "gx", 1)
    corner = jnp.concatenate([from_right, from_left])
    corner_up = send(corner, "gy", -1)
    corner_down = send(corner, "gy", 1)
    n = 2 * SLABS
    relaxed, mask, conc_new, edge = call(
        step_kernel,
        "steps",
        (f32(19, n, 8, 128), f32(18, n, 8, 128), f32(3, 8, 8, 128), f32(9, 8, 128)),
        [
            (19, n, 8, 128),
            (3, n, 8, 128),
            (2, 3, n, 8, 128),
            (n, 8, 128),
            (n, 8, 128),
            (6, n, 8, 128),
            (3, n, 8, 128),
            (n, 8, 128),
            (3, n, 8, 128),
        ],
        *kept,
        up,
        down,
        from_right,
        from_left,
        corner_up,
        corner_down,
    )
    strip = edge[8:]
    left = send(strip, "gx", 1)
    right = send(strip, "gx", -1)
    (pop_new,) = call(finish_kernel, "finish", (f32(19, 8, 8, 128),), [], relaxed, mask)
    wide = jnp.concatenate([edge, left, right])
    above = send(wide, "gy", -1)
    below = send(wide, "gy", 1)
    devices = lax.axis_size("gx") * lax.axis_size("gy")
    levels, rows = call(
        levels_kernel,
        "levels",
        (f32(ITERS, 8, 8, 128), f32(devices, 128)),
        [(ITERS, 3, 10, 8, 128), (16, 128)],
        edge,
        left,
        right,
        above,
        below,
    )
    rows = lax.all_to_all(rows, ("gx", "gy"), 0, 0, tiled=True)
    (pot_new,) = call(combine_kernel, "combine", (f32(8, 8, 128),), [], rows, levels, kept[2])
    return (pop_new, conc_new, pot_new)


def solution(mesh):
    placed = (
        P(None, None, "gy", "gx"),
        P(None, None, "gy", "gx"),
        P(None, "gy", "gx"),
        P(None, "gy", "gx"),
        P(None, "gy", "gx"),
    )
    return jax.shard_map(
        local,
        mesh=mesh,
        in_specs=placed,
        out_specs=(P(None, None, "gy", "gx"), P(None, None, "gy", "gx"), P(None, "gy", "gx")),
        check_vma=False,
    )
```

```python
import jax
import jax.numpy as jnp
from jax import lax
from jax.experimental import pallas as pl
from jax.experimental.pallas import tpu as pltpu
from jax.sharding import PartitionSpec as P

STEPS = 4
ITERS = 8

lattice_velocity = (
    (0, 0, 0),
    (0, 0, 1),
    (0, 0, -1),
    (0, 1, 0),
    (0, -1, 0),
    (1, 0, 0),
    (-1, 0, 0),
    (0, 1, 1),
    (0, -1, -1),
    (0, 1, -1),
    (0, -1, 1),
    (1, 0, 1),
    (-1, 0, -1),
    (1, 0, -1),
    (-1, 0, 1),
    (1, 1, 0),
    (-1, -1, 0),
    (1, -1, 0),
    (-1, 1, 0),
)
opposite = (0, 2, 1, 4, 3, 6, 5, 8, 7, 10, 9, 12, 11, 14, 13, 16, 15, 18, 17)
lattice_weight = (1.0 / 3.0,) + (1.0 / 18.0,) * 6 + (1.0 / 36.0,) * 12
relax_time = 1.25
force_scale = 0.05
valences = (1.0, -1.0, 2.0)
diffusivity = (0.05, 0.07, 0.03)
diag_coef = 6.0001
surface_scale = 2.0

FIELDS = 25
XT = 7
F_CONC, F_FLUID, F_POT, F_POT2 = 19, 22, 23, 24
SLABS = 9
TILE = (8, 128)


def lane_id():
    return lax.broadcasted_iota(jnp.int32, TILE, 1)


def row_id():
    return lax.broadcasted_iota(jnp.int32, TILE, 0)


def rl(v, amount):
    amount = amount % 128
    return v if amount == 0 else pltpu.roll(v, amount, 1)


def rs(v, amount):
    amount = amount % 8
    return v if amount == 0 else pltpu.roll(v, amount, 0)


def in_lanes(lane, start, width):
    return (lane >= start) & (lane < start + width)


def pack_kernel(*refs):
    sources, copies = refs[:5], refs[5:10]
    x_left, x_right, y_down, y_up, sems = refs[10:]
    moves = [
        pltpu.make_async_copy(sources[i], copies[i], sems.at[i]) for i in (0, 1, 2, 3, 4)
    ]
    for move in moves:
        move.start()
    pop, conc, pot, solid = copies[:4]
    lane, row = lane_id(), row_id()
    top = row < 4
    for move in moves:
        move.wait()

    def tile(k, z):
        if k < F_CONC:
            return pop[k, z]
        if k < F_FLUID:
            return conc[k - F_CONC, z]
        if k == F_FLUID:
            return 1.0 - solid[z].astype(jnp.float32)
        return pot[z]

    for t in range(XT):
        left = right = jnp.zeros(TILE, jnp.float32)
        for q in range(4):
            k = 4 * t + q
            if k >= FIELDS:
                continue
            inner = 4 if k == F_POT2 else 0
            for z in range(8):
                v = tile(k, z)
                at = 16 * z + 4 * q
                here = in_lanes(lane, at, 4)
                left = jnp.where(here, rl(v, at - inner), left)
                right = jnp.where(here, rl(v, at - (124 - inner)), right)
        x_left[t] = left
        x_right[t] = right
    for k in range(FIELDS):
        for pair in range(4):
            a, b = tile(k, 2 * pair), tile(k, 2 * pair + 1)
            low = jnp.where(top, a, rs(b, 4))
            high = jnp.where(top, rs(a, 4), b)
            if k == F_POT2:
                low, high = high, low
            y_down[4 * k + pair] = low
            y_up[4 * k + pair] = high


def y_shift(a, b, cy, halves=(0, 1)):
    if cy == 0:
        return a, b
    edge = row_id() == (0 if cy > 0 else 7)
    ra, rb = rs(a, cy), rs(b, cy)
    return tuple(jnp.where(edge, rb, ra) if h == 0 else jnp.where(edge, ra, rb) for h in halves)


def x_shift(v, side, z, cx):
    if cx > 0:
        return jnp.where(lane_id() == 0, rl(side, -(16 * z + 3)), rl(v, 1))
    return jnp.where(lane_id() == 127, rl(side, 127 - (16 * z + 12)), rl(v, -1))


def shifted(get, offset, own=False):
    cz, cy, cx = offset
    halves = (0,) if own else (0, 1)
    side = y_shift(get(16), get(17), cy, halves) if cx or not own else None
    out = []
    for z in range(8):
        source = (z - cz) % 8
        v = y_shift(get(2 * source), get(2 * source + 1), cy, halves)
        if cx:
            v = tuple(x_shift(v[h], side[h], source, cx) for h in halves)
        out.append(v)
    if not own:
        out.append(tuple(rl(side[h], 16 * cz + cx) for h in halves))
    return out


def step_kernel(
    pop, conc, pot, solid, sign, up, down, from_right, from_left, corner_up, corner_down,
    g, mask, conc_out, edge_out,
    f, vel, cc, fluid, pt, dpot, field, speed_up, flux,
):
    lane, row = lane_id(), row_id()
    top = row < 4
    slot = lane % 16

    def halves(k, z):
        u, d = up[4 * k + z // 2], down[4 * k + z // 2]
        if z % 2 == 0:
            return jnp.where(top, u, rs(d, 4))
        return jnp.where(top, rs(u, 4), d)

    def strip(k, tiles, low, high):
        q = k % 4
        out = jnp.where(slot < 4, rl(low, -4 * q), rl(high, 12 - 4 * q))
        for z in range(8):
            out = jnp.where(in_lanes(lane, 16 * z + 4, 4), rl(tiles[z], 16 * z + 4), out)
            out = jnp.where(in_lanes(lane, 16 * z + 8, 4), rl(tiles[z], 16 * z + 8 - 124), out)
        return out

    def load(k, own, put):
        t = k // 4
        a = [own(z) for z in range(8)]
        b = [halves(k, z) for z in range(8)]
        for z in range(8):
            put(2 * z, a[z])
            put(2 * z + 1, b[z])
        put(16, strip(k, a, from_left[t], from_right[t]))
        low = jnp.where(top, corner_up[XT + t], corner_down[XT + t])
        high = jnp.where(top, corner_up[t], corner_down[t])
        put(17, strip(k, b, low, high))

    def putter(ref, *index):
        def put(i, v):
            ref[(*index, i)] = v

        return put

    for k in range(19):
        load(k, lambda z, k=k: pop[k, z], putter(f, k))
    for k in range(3):
        load(F_CONC + k, lambda z, k=k: conc[k, z], putter(cc, 0, k))
    load(F_FLUID, lambda z: 1.0 - solid[z].astype(jnp.float32), putter(fluid))
    load(F_POT, lambda z: pot[z], putter(pt))

    for i in range(1, 19):
        moved = shifted(lambda s: fluid[s], lattice_velocity[i])
        for s in range(SLABS):
            for h in range(2):
                mask[i - 1, 2 * s + h] = moved[s][h] * fluid[2 * s + h]

    far = [halves(F_POT2, z) for z in range(8)]
    t2, q2 = F_POT2 // 4, F_POT2 % 4
    tp = F_POT // 4
    far_low = jnp.where(top, rs(corner_up[XT + tp], 4), rs(corner_down[XT + tp], 4))
    far_high = jnp.where(top, rs(corner_up[tp], 4), rs(corner_down[tp], 4))
    far.append(strip(F_POT, far, far_low, far_high))
    edge_low = (from_left[t2], jnp.where(top, corner_up[XT + t2], corner_down[XT + t2]))
    edge_high = (from_right[t2], jnp.where(top, corner_up[t2], corner_down[t2]))
    for axis in range(3):
        plus = tuple(1 if d == axis else 0 for d in range(3))
        minus = tuple(-p for p in plus)
        below = shifted(lambda s: pt[s], plus)
        above = shifted(lambda s: pt[s], minus)
        for s in range(SLABS):
            for h in range(2):
                lo, hi = below[s][h], above[s][h]
                if axis == 1 and h == 1:
                    lo = jnp.where(row == 4, rs(far[s], -3), lo)
                    hi = jnp.where(row == 3, rs(far[s], 3), hi)
                if axis == 2 and s == 8:
                    lo = jnp.where(slot == 0, rl(edge_low[h], -4 * q2 - 3), lo)
                    hi = jnp.where(slot == 15, rl(edge_high[h], 15 - 4 * q2), hi)
                    for z in range(8):
                        hi = jnp.where(lane == 16 * z + 7, rl(pt[2 * z + h], 16 * z + 3), hi)
                here = pt[2 * s + h]
                dpot[2 * axis, 2 * s + h] = here - lo
                dpot[2 * axis + 1, 2 * s + h] = hi - here
                field[axis, 2 * s + h] = (0.5 * force_scale) * (lo - hi)

    pairs = [(i, i + 1) for i in range(1, 19, 2)]

    def collide(s, now):
        v = [f[i, s] for i in range(19)]
        total = {}
        delta = {}
        for a, b in pairs:
            total[a] = v[a] + v[b]
            delta[a] = v[a] - v[b]
        density = (
            v[0]
            + ((total[1] + total[3]) + (total[5] + total[7]))
            + ((total[9] + total[11]) + (total[13] + total[15]) + total[17])
        )
        momentum = (
            (delta[5] + delta[11]) + (delta[13] + delta[15]) + delta[17],
            (delta[3] + delta[7]) + (delta[9] + delta[15]) - delta[17],
            (delta[1] + delta[7]) - (delta[9] - delta[11]) - delta[13],
        )
        open_cell = fluid[s]
        charge = open_cell * (
            valences[0] * cc[now, 0, s] + valences[1] * cc[now, 1, s] + valences[2] * cc[now, 2, s]
        )
        force = [charge * field[d, s] for d in range(3)]
        inverse = 1.0 / density
        u = [(momentum[d] + 0.5 * force[d]) * inverse for d in range(3)]
        for d in range(3):
            vel[d, s] = u[d]
        speed = u[0] * u[0] + u[1] * u[1] + u[2] * u[2]
        work = u[0] * force[0] + u[1] * force[1] + u[2] * force[2]
        flow = [density * u[d] for d in range(3)]
        keep = 1.0 - 1.0 / relax_time
        gain = 1.0 / relax_time
        push = 1.0 - 0.5 / relax_time
        base = gain * density - (1.5 * gain) * (density * speed) - (3.0 * push) * work
        odd = [(3.0 * gain) * flow[d] + (3.0 * push) * force[d] for d in range(3)]
        even = [(4.5 * gain) * flow[d] + (9.0 * push) * force[d] for d in range(3)]
        is_open = open_cell > 0.5
        g[0, s] = jnp.where(is_open, keep * v[0] + lattice_weight[0] * base, v[0])

        def along(c, vector):
            running = None
            for d in range(3):
                if c[d] != 0:
                    if running is None:
                        running = vector[d] if c[d] > 0 else -vector[d]
                    else:
                        running = running + vector[d] if c[d] > 0 else running - vector[d]
            return running

        for a, b in pairs:
            c, w = lattice_velocity[a], lattice_weight[a]
            middle = base + along(c, u) * along(c, even)
            side = along(c, odd)
            g[a, s] = jnp.where(is_open, keep * v[a] + w * (middle + side), v[b])
            g[b, s] = jnp.where(is_open, keep * v[b] + w * (middle - side), v[a])

    def collide_all(now):
        def both(s, c):
            collide(2 * s, now)
            collide(2 * s + 1, now)
            return c

        lax.fori_loop(0, SLABS, both, 0)

    def stream():
        for s in range(2 * SLABS):
            f[0, s] = g[0, s]
        for i in range(1, 19):
            moved = shifted(lambda s, i=i: g[i, s], lattice_velocity[i])
            for s in range(SLABS):
                for h in range(2):
                    n = 2 * s + h
                    f[i, n] = jnp.where(mask[i - 1, n] > 0.5, moved[s][h], g[opposite[i], n])

    def ions(now, after, own=False):
        for axis in range(3):
            plus = tuple(1 if d == axis else 0 for d in range(3))
            minus = tuple(-p for p in plus)
            upper = 2 * (2 - axis) + 1
            v_high = shifted(lambda s: vel[axis, s], minus)
            for s in range(SLABS):
                for h in range(2):
                    n = 2 * s + h
                    speed_up[n] = 0.25 * (vel[axis, n] + v_high[s][h])
            for k in range(3):
                c_high = shifted(lambda s: cc[now, k, s], minus)
                rate = diffusivity[k]
                drift = 0.5 * rate * valences[k]
                for s in range(SLABS):
                    for h in range(2):
                        n = 2 * s + h
                        here, hi = cc[now, k, n], c_high[s][h]
                        pull = speed_up[n] - drift * dpot[2 * axis + 1, n]
                        flux[k, n] = mask[upper, n] * (rate * (here - hi) + (here + hi) * pull)
                low = shifted(lambda s: flux[k, s], plus, own)
                for s in range(8 if own else SLABS):
                    for h in range(1 if own else 2):
                        n = 2 * s + h
                        before = cc[now if axis == 0 else after, k, n]
                        cc[after, k, n] = before - (flux[k, n] - low[s][h])

    def one_step(step, carry):
        now = lax.rem(step, 2)
        collide_all(now)
        stream()
        ions(now, 1 - now)
        return carry

    lax.fori_loop(0, STEPS - 1, one_step, 0)
    final = (STEPS - 1) % 2
    collide_all(final)
    ions(final, 1 - final, own=True)

    last = STEPS % 2
    edge = jnp.zeros(TILE, jnp.float32)
    for z in range(8):
        n = 2 * z
        c = [cc[last, k, n] for k in range(3)]
        for k in range(3):
            conc_out[k, z] = c[k]
        open_cell = fluid[n]
        target = open_cell * (
            valences[0] * c[0] + valences[1] * c[1] + valences[2] * c[2]
        ) + surface_scale * sign[z].astype(jnp.float32) * (1.0 - open_cell)
        spread = (
            (dpot[1, n] - dpot[0, n]) + (dpot[3, n] - dpot[2, n]) + (dpot[5, n] - dpot[4, n])
        )
        residual = target - ((diag_coef - 6.0) * pt[n] - spread)
        edge_out[z] = residual
        edge = jnp.where(in_lanes(lane, 16 * z, 8), rl(residual, 16 * z - 120), edge)
        edge = jnp.where(in_lanes(lane, 16 * z + 8, 8), rl(residual, 16 * z + 8), edge)
    edge_out[8] = edge


def finish_kernel(g, mask, pop_out):
    for z in range(8):
        pop_out[0, z] = g[0, 2 * z]
    for i in range(1, 19):
        moved = shifted(lambda s, i=i: g[i, s], lattice_velocity[i], own=True)
        for z in range(8):
            pop_out[i, z] = jnp.where(mask[i - 1, 2 * z] > 0.5, moved[z][0], g[opposite[i], 2 * z])


def levels_kernel(own, left, right, up, down, level_out, row_out, lv, part):
    lane, row = lane_id(), row_id()
    slot = lane % 16
    first_row, last_row = row == 0, row == 7
    first_lane, last_lane = lane == 0, lane == 127
    sources = (
        (own, left[0], right[0]),
        (up, up[9], up[10]),
        (down, down[9], down[10]),
    )
    for r, (main, low, high) in enumerate(sources):
        for s in range(8):
            lv[0, r, s] = main[s]
        lv[0, r, 8] = jnp.where(slot < 8, low, main[8])
        lv[0, r, 9] = jnp.where(slot < 8, main[8], high)

    def around(j, r, s, low, high):
        v = lv[j, r, s]
        above, below = lv[j, (r + 1) % 3, s], lv[j, (r + 2) % 3, s]
        vertical = jnp.where(last_row, rs(above, -1), rs(v, -1)) + jnp.where(
            first_row, rs(below, 1), rs(v, 1)
        )
        if s < 8:
            across = jnp.where(first_lane, rl(low, -(16 * s + 7)), rl(v, 1)) + jnp.where(
                last_lane, rl(high, 127 - (16 * s + 8)), rl(v, -1)
            )
            return (lv[j, r, (s + 1) % 8] + lv[j, r, (s - 1) % 8]) + vertical + across
        return (rl(v, 16) + rl(v, -16)) + vertical + (rl(v, 1) + rl(v, -1))

    for j in range(ITERS):
        done = j == ITERS - 1
        squares = products = jnp.zeros(TILE, jnp.float32)
        for r in range(1 if done else 3):
            low, high = lv[j, r, 8], lv[j, r, 9]
            for s in range(8 if done else 10):
                total = around(j, r, s, low, high)
                if j == 0:
                    fresh = -total / 6.0
                else:
                    fresh = total * (-1.0 / 3.0) - lv[j - 1, r, s]
                if not done:
                    lv[j + 1, r, s] = fresh
                if r == 0 and s < 8:
                    here = lv[j, 0, s]
                    level_out[j, s] = here
                    squares = squares + here * here
                    products = products + here * fresh
        part[j : j + 1, :] = jnp.sum(squares, axis=0, keepdims=True)
        part[8 + j : 9 + j, :] = jnp.sum(products, axis=0, keepdims=True)
    sums = jnp.sum(part[...], axis=1, keepdims=True)
    diagonal = lax.broadcasted_iota(jnp.int32, (16, 128), 0) == lax.broadcasted_iota(
        jnp.int32, (16, 128), 1
    )
    one_row = jnp.sum(jnp.where(diagonal, sums, 0.0), axis=0, keepdims=True)
    row_out[...] = jnp.broadcast_to(one_row, row_out.shape)


def combine_kernel(rows, levels, pot, out):
    total = jnp.broadcast_to(jnp.sum(rows[...], axis=0, keepdims=True), (16, 128))
    diagonal = lax.broadcasted_iota(jnp.int32, (16, 128), 0) == lax.broadcasted_iota(
        jnp.int32, (16, 128), 1
    )
    sums = jnp.sum(jnp.where(diagonal, total, 0.0), axis=1, keepdims=True)

    def entry(i):
        return jnp.broadcast_to(sums[i : i + 1, :], TILE)

    moment = [None] * 16
    moment[0], moment[1] = entry(0), entry(8)
    for k in range(1, ITERS):
        moment[2 * k] = 2.0 * entry(k) - moment[0]
        moment[2 * k + 1] = 2.0 * entry(8 + k) - moment[1]
    gram = {}
    for i in range(ITERS + 1):
        for j in range(i, ITERS + 1):
            if i + j < 16:
                gram[i, j] = gram[j, i] = 0.5 * (moment[i + j] + moment[j - i])

    def inner(a, b):
        running = None
        for i, x in enumerate(a):
            row = None
            for j, y in enumerate(b):
                term = gram[i, j] * y
                row = term if row is None else row + term
            row = x * row
            running = row if running is None else running + row
        return running

    one, zero = jnp.ones(TILE, jnp.float32), jnp.zeros(TILE, jnp.float32)
    search, rest, found = [one], [one], []
    left = moment[0]
    for k in range(ITERS):
        image = [zero] * (k + 2)
        for j in range(k + 1):
            image[j] = image[j] + diag_coef * search[j]
            if j == 0:
                image[1] = image[1] + 6.0 * search[0]
            else:
                image[j + 1] = image[j + 1] + 3.0 * search[j]
                image[j - 1] = image[j - 1] + 3.0 * search[j]
        length = left / inner(search, image)
        found = [
            (found[j] if j < len(found) else zero) + length * search[j] for j in range(k + 1)
        ]
        if k == ITERS - 1:
            break
        rest = [(rest[j] if j < k + 1 else zero) - length * image[j] for j in range(k + 2)]
        fresh = inner(rest, rest)
        ratio = fresh / left
        search = [rest[j] + (ratio * search[j] if j < k + 1 else zero) for j in range(k + 2)]
        left = fresh
    for z in range(8):
        running = found[0] * levels[0, z]
        for j in range(1, ITERS):
            running = running + found[j] * levels[j, z]
        out[z] = pot[z] + running


def in_vmem(count):
    return [pl.BlockSpec(memory_space=pltpu.VMEM)] * count


def f32(*shape):
    return jax.ShapeDtypeStruct(shape, jnp.float32)


def call(kernel, name, outs, scratch, *args, in_specs=None):
    return pl.pallas_call(
        kernel,
        name=name,
        out_shape=outs,
        in_specs=in_specs or in_vmem(len(args)),
        out_specs=in_vmem(len(outs)),
        scratch_shapes=[
            pltpu.VMEM(shape, jnp.float32) if isinstance(shape, tuple) else shape
            for shape in scratch
        ],
        compiler_params=pltpu.CompilerParams(vmem_limit_bytes=48 << 20),
    )(*args)


def send(block, axis, step):
    count = lax.axis_size(axis)
    return lax.ppermute(block, axis, [(i, (i + step) % count) for i in range(count)])


def local(populations, concentrations, potential, solid_mask, surface_sign):
    inputs = tuple(
        pltpu.with_memory_space_constraint(a, pltpu.HBM)
        for a in (populations, concentrations, potential, solid_mask, surface_sign)
    )
    packed = call(
        pack_kernel,
        "pack",
        tuple(jax.ShapeDtypeStruct(a.shape, a.dtype) for a in inputs)
        + (f32(XT, 8, 128), f32(XT, 8, 128), f32(4 * FIELDS, 8, 128), f32(4 * FIELDS, 8, 128)),
        [pltpu.SemaphoreType.DMA((5,))],
        *inputs,
        in_specs=[pl.BlockSpec(memory_space=pltpu.HBM)] * 5,
    )
    kept, (x_left, x_right, y_down, y_up) = packed[:5], packed[5:]
    up = send(y_down, "gy", -1)
    down = send(y_up, "gy", 1)
    from_right = send(x_left, "gx", -1)
    from_left = send(x_right, "gx", 1)
    corner = jnp.concatenate([from_right, from_left])
    corner_up = send(corner, "gy", -1)
    corner_down = send(corner, "gy", 1)
    n = 2 * SLABS
    relaxed, mask, conc_new, edge = call(
        step_kernel,
        "steps",
        (f32(19, n, 8, 128), f32(18, n, 8, 128), f32(3, 8, 8, 128), f32(9, 8, 128)),
        [
            (19, n, 8, 128),
            (3, n, 8, 128),
            (2, 3, n, 8, 128),
            (n, 8, 128),
            (n, 8, 128),
            (6, n, 8, 128),
            (3, n, 8, 128),
            (n, 8, 128),
            (3, n, 8, 128),
        ],
        *kept,
        up,
        down,
        from_right,
        from_left,
        corner_up,
        corner_down,
    )
    strip = edge[8:]
    left = send(strip, "gx", 1)
    right = send(strip, "gx", -1)
    (pop_new,) = call(finish_kernel, "finish", (f32(19, 8, 8, 128),), [], relaxed, mask)
    left, right, pop_new = lax.optimization_barrier((left, right, pop_new))
    wide = jnp.concatenate([edge, left, right])
    above = send(wide, "gy", -1)
    below = send(wide, "gy", 1)
    devices = lax.axis_size("gx") * lax.axis_size("gy")
    levels, rows = call(
        levels_kernel,
        "levels",
        (f32(ITERS, 8, 8, 128), f32(devices, 128)),
        [(ITERS, 3, 10, 8, 128), (16, 128)],
        edge,
        left,
        right,
        above,
        below,
    )
    rows = lax.all_to_all(rows, ("gx", "gy"), 0, 0, tiled=True)
    (pot_new,) = call(combine_kernel, "combine", (f32(8, 8, 128),), [], rows, levels, kept[2])
    return (pop_new, conc_new, pot_new)


def solution(mesh):
    placed = (
        P(None, None, "gy", "gx"),
        P(None, None, "gy", "gx"),
        P(None, "gy", "gx"),
        P(None, "gy", "gx"),
        P(None, "gy", "gx"),
    )
    return jax.shard_map(
        local,
        mesh=mesh,
        in_specs=placed,
        out_specs=(P(None, None, "gy", "gx"), P(None, None, "gy", "gx"), P(None, "gy", "gx")),
        check_vma=False,
    )
```

```python
import jax
import jax.numpy as jnp
from jax import lax
from jax.experimental import pallas as pl
from jax.experimental.pallas import tpu as pltpu
from jax.sharding import PartitionSpec as P

STEPS = 4
ITERS = 8

lattice_velocity = (
    (0, 0, 0),
    (0, 0, 1),
    (0, 0, -1),
    (0, 1, 0),
    (0, -1, 0),
    (1, 0, 0),
    (-1, 0, 0),
    (0, 1, 1),
    (0, -1, -1),
    (0, 1, -1),
    (0, -1, 1),
    (1, 0, 1),
    (-1, 0, -1),
    (1, 0, -1),
    (-1, 0, 1),
    (1, 1, 0),
    (-1, -1, 0),
    (1, -1, 0),
    (-1, 1, 0),
)
opposite = (0, 2, 1, 4, 3, 6, 5, 8, 7, 10, 9, 12, 11, 14, 13, 16, 15, 18, 17)
lattice_weight = (1.0 / 3.0,) + (1.0 / 18.0,) * 6 + (1.0 / 36.0,) * 12
relax_time = 1.25
force_scale = 0.05
valences = (1.0, -1.0, 2.0)
diffusivity = (0.05, 0.07, 0.03)
diag_coef = 6.0001
surface_scale = 2.0

FIELDS = 25
XT = 7
F_CONC, F_FLUID, F_POT, F_POT2 = 19, 22, 23, 24
SLABS = 9
TILE = (8, 128)


def lane_id():
    return lax.broadcasted_iota(jnp.int32, TILE, 1)


def row_id():
    return lax.broadcasted_iota(jnp.int32, TILE, 0)


def rl(v, amount):
    amount = amount % 128
    return v if amount == 0 else pltpu.roll(v, amount, 1)


def rs(v, amount):
    amount = amount % 8
    return v if amount == 0 else pltpu.roll(v, amount, 0)


def in_lanes(lane, start, width):
    return (lane >= start) & (lane < start + width)


def pack_kernel(*refs):
    sources, copies = refs[:5], refs[5:10]
    x_left, x_right, y_down, y_up, sems = refs[10:]
    moves = [
        pltpu.make_async_copy(sources[i], copies[i], sems.at[i]) for i in (0, 1, 2, 3, 4)
    ]
    for move in moves:
        move.start()
    pop, conc, pot, solid = copies[:4]
    lane, row = lane_id(), row_id()
    top = row < 4
    for move in moves:
        move.wait()

    def tile(k, z):
        if k < F_CONC:
            return pop[k, z]
        if k < F_FLUID:
            return conc[k - F_CONC, z]
        if k == F_FLUID:
            return 1.0 - solid[z].astype(jnp.float32)
        return pot[z]

    for t in range(XT):
        left = right = jnp.zeros(TILE, jnp.float32)
        for q in range(4):
            k = 4 * t + q
            if k >= FIELDS:
                continue
            inner = 4 if k == F_POT2 else 0
            for z in range(8):
                v = tile(k, z)
                at = 16 * z + 4 * q
                here = in_lanes(lane, at, 4)
                left = jnp.where(here, rl(v, at - inner), left)
                right = jnp.where(here, rl(v, at - (124 - inner)), right)
        x_left[t] = left
        x_right[t] = right
    for k in range(FIELDS):
        for pair in range(4):
            a, b = tile(k, 2 * pair), tile(k, 2 * pair + 1)
            low = jnp.where(top, a, rs(b, 4))
            high = jnp.where(top, rs(a, 4), b)
            if k == F_POT2:
                low, high = high, low
            y_down[4 * k + pair] = low
            y_up[4 * k + pair] = high


def y_shift(a, b, cy, halves=(0, 1)):
    if cy == 0:
        return a, b
    edge = row_id() == (0 if cy > 0 else 7)
    ra, rb = rs(a, cy), rs(b, cy)
    return tuple(jnp.where(edge, rb, ra) if h == 0 else jnp.where(edge, ra, rb) for h in halves)


def x_shift(v, side, z, cx):
    if cx > 0:
        return jnp.where(lane_id() == 0, rl(side, -(16 * z + 3)), rl(v, 1))
    return jnp.where(lane_id() == 127, rl(side, 127 - (16 * z + 12)), rl(v, -1))


def shifted(get, offset, own=False):
    cz, cy, cx = offset
    halves = (0,) if own else (0, 1)
    side = y_shift(get(16), get(17), cy, halves) if cx or not own else None
    out = []
    for z in range(8):
        source = (z - cz) % 8
        v = y_shift(get(2 * source), get(2 * source + 1), cy, halves)
        if cx:
            v = tuple(x_shift(v[h], side[h], source, cx) for h in halves)
        out.append(v)
    if not own:
        out.append(tuple(rl(side[h], 16 * cz + cx) for h in halves))
    return out


def shifted_slab(get, offset, s):
    cz, cy, cx = offset
    if s == 8:
        v = y_shift(get(16), get(17), cy)
        return tuple(rl(x, 16 * cz + cx) for x in v)
    source = (s - cz) % 8
    v = y_shift(get(2 * source), get(2 * source + 1), cy)
    if cx:
        side = y_shift(get(16), get(17), cy)
        v = tuple(x_shift(v[h], side[h], source, cx) for h in range(2))
    return v


def step_kernel(
    pop, conc, pot, solid, sign, x_left, x_right, up, down, from_right, from_left, corner_up,
    corner_down, g, mask, conc_out, edge_out,
    f, below_rows, vel, cc, cn, fluid, pt, dpot, field, flux,
):
    lane, row = lane_id(), row_id()
    top = row < 4
    slot = lane % 16

    def halves(k, z):
        u, d = up[4 * k + z // 2], down[4 * k + z // 2]
        if z % 2 == 0:
            return jnp.where(top, u, rs(d, 4))
        return jnp.where(top, rs(u, 4), d)

    def strip(k, tiles, low, high):
        q = k % 4
        out = jnp.where(slot < 4, rl(low, -4 * q), rl(high, 12 - 4 * q))
        for z in range(8):
            out = jnp.where(in_lanes(lane, 16 * z + 4, 4), rl(tiles[z], 16 * z + 4), out)
            out = jnp.where(in_lanes(lane, 16 * z + 8, 4), rl(tiles[z], 16 * z + 8 - 124), out)
        return out

    def strips(k, b):
        t = k // 4
        low = jnp.where(top, corner_up[XT + t], corner_down[XT + t])
        high = jnp.where(top, corner_up[t], corner_down[t])
        q = k % 4
        mine = jnp.where(
            slot < 8,
            jnp.where(slot < 4, rl(from_left[t], -4 * q), rl(x_left[t], 4 - 4 * q)),
            jnp.where(slot < 12, rl(x_right[t], 8 - 4 * q), rl(from_right[t], 12 - 4 * q)),
        )
        return mine, strip(k, b, low, high)

    def load(k, own, put):
        a = [own(z) for z in range(8)]
        b = [halves(k, z) for z in range(8)]
        for z in range(8):
            put(2 * z, a[z])
            put(2 * z + 1, b[z])
        sa, sb = strips(k, b)
        put(16, sa)
        put(17, sb)

    def putter(ref, *index):
        def put(i, v):
            ref[(*index, i)] = v

        return put

    for k in range(3):
        load(F_CONC + k, lambda z, k=k: conc[k, z], putter(cc, k))
    load(F_FLUID, lambda z: 1.0 - solid[z].astype(jnp.float32), putter(fluid))
    load(F_POT, lambda z: pot[z], putter(pt))

    for i in range(1, 19):
        moved = shifted(lambda s: fluid[s], lattice_velocity[i])
        for s in range(SLABS):
            for h in range(2):
                mask[i - 1, 2 * s + h] = moved[s][h] * fluid[2 * s + h]

    far = [halves(F_POT2, z) for z in range(8)]
    t2, q2 = F_POT2 // 4, F_POT2 % 4
    tp = F_POT // 4
    far_low = jnp.where(top, rs(corner_up[XT + tp], 4), rs(corner_down[XT + tp], 4))
    far_high = jnp.where(top, rs(corner_up[tp], 4), rs(corner_down[tp], 4))
    far.append(strip(F_POT, far, far_low, far_high))
    edge_low = (from_left[t2], jnp.where(top, corner_up[XT + t2], corner_down[XT + t2]))
    edge_high = (from_right[t2], jnp.where(top, corner_up[t2], corner_down[t2]))
    for axis in range(3):
        plus = tuple(1 if d == axis else 0 for d in range(3))
        minus = tuple(-p for p in plus)
        below = shifted(lambda s: pt[s], plus)
        above = shifted(lambda s: pt[s], minus)
        for s in range(SLABS):
            for h in range(2):
                lo, hi = below[s][h], above[s][h]
                if axis == 1 and h == 1:
                    lo = jnp.where(row == 4, rs(far[s], -3), lo)
                    hi = jnp.where(row == 3, rs(far[s], 3), hi)
                if axis == 2 and s == 8:
                    lo = jnp.where(slot == 0, rl(edge_low[h], -4 * q2 - 3), lo)
                    hi = jnp.where(slot == 15, rl(edge_high[h], 15 - 4 * q2), hi)
                    for z in range(8):
                        hi = jnp.where(lane == 16 * z + 7, rl(pt[2 * z + h], 16 * z + 3), hi)
                here = pt[2 * s + h]
                if h == 0 and s < 8:
                    dpot[3 + axis, 2 * s] = here - lo
                dpot[axis, 2 * s + h] = hi - here
                field[axis, 2 * s + h] = (0.5 * force_scale) * (lo - hi)

    pairs = [(i, i + 1) for i in range(1, 19, 2)]

    def along(c, vector):
        running = None
        for d in range(3):
            if c[d] != 0:
                if running is None:
                    running = vector[d] if c[d] > 0 else -vector[d]
                else:
                    running = running + vector[d] if c[d] > 0 else running - vector[d]
        return running

    def collide(s, v):
        total = {}
        delta = {}
        for a, b in pairs:
            total[a] = v[a] + v[b]
            delta[a] = v[a] - v[b]
        density = (
            v[0]
            + ((total[1] + total[3]) + (total[5] + total[7]))
            + ((total[9] + total[11]) + (total[13] + total[15]) + total[17])
        )
        momentum = (
            (delta[5] + delta[11]) + (delta[13] + delta[15]) + delta[17],
            (delta[3] + delta[7]) + (delta[9] + delta[15]) - delta[17],
            (delta[1] + delta[7]) - (delta[9] - delta[11]) - delta[13],
        )
        open_cell = fluid[s]
        charge = open_cell * (
            valences[0] * cc[0, s] + valences[1] * cc[1, s] + valences[2] * cc[2, s]
        )
        force = [charge * field[d, s] for d in range(3)]
        inverse = 1.0 / density
        u = [(momentum[d] + 0.5 * force[d]) * inverse for d in range(3)]
        for d in range(3):
            vel[d, s] = u[d]
        speed = u[0] * u[0] + u[1] * u[1] + u[2] * u[2]
        work = u[0] * force[0] + u[1] * force[1] + u[2] * force[2]
        flow = [density * u[d] for d in range(3)]
        keep = 1.0 - 1.0 / relax_time
        gain = 1.0 / relax_time
        push = 1.0 - 0.5 / relax_time
        base = gain * density - (1.5 * gain) * (density * speed) - (3.0 * push) * work
        odd = [(3.0 * gain) * flow[d] + (3.0 * push) * force[d] for d in range(3)]
        even = [(4.5 * gain) * flow[d] + (9.0 * push) * force[d] for d in range(3)]
        is_open = open_cell > 0.5
        g[0, s] = jnp.where(is_open, keep * v[0] + lattice_weight[0] * base, v[0])
        for a, b in pairs:
            c, w = lattice_velocity[a], lattice_weight[a]
            middle = base + along(c, u) * along(c, even)
            side = along(c, odd)
            g[a, s] = jnp.where(is_open, keep * v[a] + w * (middle + side), v[b])
            g[b, s] = jnp.where(is_open, keep * v[b] + w * (middle - side), v[a])

    for z in range(8):
        collide(2 * z, [pop[k, z] for k in range(19)])
    for z in range(8):
        v = [halves(k, z) for k in range(19)]
        for k in range(19):
            below_rows[k, z] = v[k]
        collide(2 * z + 1, v)
    both = [
        strips(k, [below_rows[k, z] for z in range(8)])
        for k in range(19)
    ]
    for h in range(2):
        collide(16 + h, [both[k][h] for k in range(19)])

    def stream():
        for s in range(2 * SLABS):
            f[0, s] = g[0, s]
        for s in range(SLABS):
            for i in range(1, 19):
                moved = shifted_slab(lambda n, i=i: g[i, n], lattice_velocity[i], s)
                for h in range(2):
                    n = 2 * s + h
                    f[i, n] = jnp.where(mask[i - 1, n] > 0.5, moved[h], g[opposite[i], n])
        for s in range(2 * SLABS):
            collide(s, [f[i, s] for i in range(19)])

    def ions(own=False):
        for axis in range(3):
            plus = tuple(1 if d == axis else 0 for d in range(3))
            minus = tuple(-p for p in plus)
            upper = 2 * (2 - axis) + 1
            for s in [8] + list(range(8)):
                v_high = shifted_slab(lambda n: vel[axis, n], minus, s)
                c_high = [shifted_slab(lambda n, k=k: cc[k, n], minus, s) for k in range(3)]
                for h in range(2):
                    n = 2 * s + h
                    speed = 0.25 * (vel[axis, n] + v_high[h])
                    step, is_open = dpot[axis, n], mask[upper, n]
                    for k in range(3):
                        rate = diffusivity[k]
                        here, hi = cc[k, n], c_high[k][h]
                        pull = speed - (0.5 * rate * valences[k]) * step
                        flux[axis, k, n] = is_open * (rate * (here - hi) + (here + hi) * pull)
        for k in range(3):
            for s in range(8 if own else SLABS):
                low = [
                    shifted_slab(
                        lambda n, d=d: flux[d, k, n], tuple(1 if e == d else 0 for e in range(3)), s
                    )
                    for d in range(3)
                ]
                for h in range(1 if own else 2):
                    n = 2 * s + h
                    net = [flux[d, k, n] - low[d][h] for d in range(3)]
                    cn[k, n] = cc[k, n] - ((net[0] + net[1]) + net[2])

    def one_step(step, carry):
        ions()
        for k in range(3):
            for n in range(2 * SLABS):
                cc[k, n] = cn[k, n]
        stream()
        return carry

    lax.fori_loop(0, STEPS - 1, one_step, 0)
    ions(own=True)

    edge = jnp.zeros(TILE, jnp.float32)
    for z in range(8):
        n = 2 * z
        c = [cn[k, n] for k in range(3)]
        for k in range(3):
            conc_out[k, z] = c[k]
        open_cell = fluid[n]
        target = open_cell * (
            valences[0] * c[0] + valences[1] * c[1] + valences[2] * c[2]
        ) + surface_scale * sign[z].astype(jnp.float32) * (1.0 - open_cell)
        spread = (
            (dpot[0, n] - dpot[3, n]) + (dpot[1, n] - dpot[4, n]) + (dpot[2, n] - dpot[5, n])
        )
        residual = target - ((diag_coef - 6.0) * pt[n] - spread)
        edge_out[z] = residual
        edge = jnp.where(in_lanes(lane, 16 * z, 8), rl(residual, 16 * z - 120), edge)
        edge = jnp.where(in_lanes(lane, 16 * z + 8, 8), rl(residual, 16 * z + 8), edge)
    edge_out[8] = edge


STEP_SHAPES = (
    (
        (19, 2 * SLABS, 8, 128),
        (18, 2 * SLABS, 8, 128),
        (3, 8, 8, 128),
        (9, 8, 128),
    ),
    (
        (19, 2 * SLABS, 8, 128),
        (19, 8, 8, 128),
        (3, 2 * SLABS, 8, 128),
        (3, 2 * SLABS, 8, 128),
        (3, 2 * SLABS, 8, 128),
        (2 * SLABS, 8, 128),
        (2 * SLABS, 8, 128),
        (6, 2 * SLABS, 8, 128),
        (3, 2 * SLABS, 8, 128),
        (3, 3, 2 * SLABS, 8, 128),
    ),
)


def finish_kernel(g, mask, pop_out):
    for z in range(8):
        pop_out[0, z] = g[0, 2 * z]
    for i in range(1, 19):
        moved = shifted(lambda s, i=i: g[i, s], lattice_velocity[i], own=True)
        for z in range(8):
            pop_out[i, z] = jnp.where(
                mask[i - 1, 2 * z] > 0.5, moved[z][0], g[opposite[i], 2 * z]
            )


def levels_kernel(own, left, right, up, down, level_out, row_out, lv, part):
    lane, row = lane_id(), row_id()
    slot = lane % 16
    first_row, last_row = row == 0, row == 7
    first_lane, last_lane = lane == 0, lane == 127
    sources = (
        (own, left[0], right[0]),
        (up, up[9], up[10]),
        (down, down[9], down[10]),
    )
    for r, (main, low, high) in enumerate(sources):
        for s in range(8):
            lv[0, r, s] = main[s]
        lv[0, r, 8] = jnp.where(slot < 8, low, main[8])
        lv[0, r, 9] = jnp.where(slot < 8, main[8], high)

    def around(j, r, s, low, high):
        v = lv[j, r, s]
        above, below = lv[j, (r + 1) % 3, s], lv[j, (r + 2) % 3, s]
        vertical = jnp.where(last_row, rs(above, -1), rs(v, -1)) + jnp.where(
            first_row, rs(below, 1), rs(v, 1)
        )
        if s < 8:
            across = jnp.where(first_lane, rl(low, -(16 * s + 7)), rl(v, 1)) + jnp.where(
                last_lane, rl(high, 127 - (16 * s + 8)), rl(v, -1)
            )
            return (lv[j, r, (s + 1) % 8] + lv[j, r, (s - 1) % 8]) + vertical + across
        return (rl(v, 16) + rl(v, -16)) + vertical + (rl(v, 1) + rl(v, -1))

    for j in range(ITERS):
        done = j == ITERS - 1
        squares = products = jnp.zeros(TILE, jnp.float32)
        for r in range(1 if done else 3):
            low, high = lv[j, r, 8], lv[j, r, 9]
            for s in range(8 if done else 10):
                total = around(j, r, s, low, high)
                if j == 0:
                    fresh = -total / 6.0
                else:
                    fresh = total * (-1.0 / 3.0) - lv[j - 1, r, s]
                if not done:
                    lv[j + 1, r, s] = fresh
                if r == 0 and s < 8:
                    here = lv[j, 0, s]
                    level_out[j, s] = here
                    squares = squares + here * here
                    products = products + here * fresh
        part[j : j + 1, :] = jnp.sum(squares, axis=0, keepdims=True)
        part[8 + j : 9 + j, :] = jnp.sum(products, axis=0, keepdims=True)
    sums = jnp.sum(part[...], axis=1, keepdims=True)
    diagonal = lax.broadcasted_iota(jnp.int32, (16, 128), 0) == lax.broadcasted_iota(
        jnp.int32, (16, 128), 1
    )
    one_row = jnp.sum(jnp.where(diagonal, sums, 0.0), axis=0, keepdims=True)
    row_out[...] = jnp.broadcast_to(one_row, row_out.shape)


def combine_kernel(rows, levels, pot, out):
    total = jnp.broadcast_to(jnp.sum(rows[...], axis=0, keepdims=True), (16, 128))
    diagonal = lax.broadcasted_iota(jnp.int32, (16, 128), 0) == lax.broadcasted_iota(
        jnp.int32, (16, 128), 1
    )
    sums = jnp.sum(jnp.where(diagonal, total, 0.0), axis=1, keepdims=True)

    def entry(i):
        return jnp.broadcast_to(sums[i : i + 1, :], TILE)

    moment = [None] * 16
    moment[0], moment[1] = entry(0), entry(8)
    for k in range(1, ITERS):
        moment[2 * k] = 2.0 * entry(k) - moment[0]
        moment[2 * k + 1] = 2.0 * entry(8 + k) - moment[1]
    gram = {}
    for i in range(ITERS + 1):
        for j in range(i, ITERS + 1):
            if i + j < 16:
                gram[i, j] = gram[j, i] = 0.5 * (moment[i + j] + moment[j - i])

    def inner(a, b):
        running = None
        for i, x in enumerate(a):
            row = None
            for j, y in enumerate(b):
                term = gram[i, j] * y
                row = term if row is None else row + term
            row = x * row
            running = row if running is None else running + row
        return running

    one, zero = jnp.ones(TILE, jnp.float32), jnp.zeros(TILE, jnp.float32)
    search, rest, found = [one], [one], []
    left = moment[0]
    for k in range(ITERS):
        image = [zero] * (k + 2)
        for j in range(k + 1):
            image[j] = image[j] + diag_coef * search[j]
            if j == 0:
                image[1] = image[1] + 6.0 * search[0]
            else:
                image[j + 1] = image[j + 1] + 3.0 * search[j]
                image[j - 1] = image[j - 1] + 3.0 * search[j]
        length = left / inner(search, image)
        found = [
            (found[j] if j < len(found) else zero) + length * search[j] for j in range(k + 1)
        ]
        if k == ITERS - 1:
            break
        rest = [(rest[j] if j < k + 1 else zero) - length * image[j] for j in range(k + 2)]
        fresh = inner(rest, rest)
        ratio = fresh / left
        search = [rest[j] + (ratio * search[j] if j < k + 1 else zero) for j in range(k + 2)]
        left = fresh
    for z in range(8):
        running = found[0] * levels[0, z]
        for j in range(1, ITERS):
            running = running + found[j] * levels[j, z]
        out[z] = pot[z] + running


def in_vmem(count):
    return [pl.BlockSpec(memory_space=pltpu.VMEM)] * count


def f32(*shape):
    return jax.ShapeDtypeStruct(shape, jnp.float32)


def call(kernel, name, outs, scratch, *args, in_specs=None):
    return pl.pallas_call(
        kernel,
        name=name,
        out_shape=outs,
        in_specs=in_specs or in_vmem(len(args)),
        out_specs=in_vmem(len(outs)),
        scratch_shapes=[
            pltpu.VMEM(shape, jnp.float32) if isinstance(shape, tuple) else shape
            for shape in scratch
        ],
        compiler_params=pltpu.CompilerParams(vmem_limit_bytes=48 << 20),
    )(*args)


def send(block, axis, step):
    count = lax.axis_size(axis)
    return lax.ppermute(block, axis, [(i, (i + step) % count) for i in range(count)])


def local(populations, concentrations, potential, solid_mask, surface_sign):
    inputs = tuple(
        pltpu.with_memory_space_constraint(a, pltpu.HBM)
        for a in (populations, concentrations, potential, solid_mask, surface_sign)
    )
    packed = call(
        pack_kernel,
        "pack",
        tuple(jax.ShapeDtypeStruct(a.shape, a.dtype) for a in inputs)
        + (f32(XT, 8, 128), f32(XT, 8, 128), f32(4 * FIELDS, 8, 128), f32(4 * FIELDS, 8, 128)),
        [pltpu.SemaphoreType.DMA((5,))],
        *inputs,
        in_specs=[pl.BlockSpec(memory_space=pltpu.HBM)] * 5,
    )
    kept, (x_left, x_right, y_down, y_up) = packed[:5], packed[5:]
    up = send(y_down, "gy", -1)
    down = send(y_up, "gy", 1)
    from_right = send(x_left, "gx", -1)
    from_left = send(x_right, "gx", 1)
    corner = jnp.concatenate([from_right, from_left])
    corner_up = send(corner, "gy", -1)
    corner_down = send(corner, "gy", 1)
    relaxed, mask, conc_new, edge = call(
        step_kernel,
        "steps",
        tuple(f32(*shape) for shape in STEP_SHAPES[0]),
        STEP_SHAPES[1],
        *kept,
        x_left,
        x_right,
        up,
        down,
        from_right,
        from_left,
        corner_up,
        corner_down,
    )
    strip = edge[8:]
    left = send(strip, "gx", 1)
    right = send(strip, "gx", -1)
    (pop_new,) = call(finish_kernel, "finish", (f32(19, 8, 8, 128),), [], relaxed, mask)
    left, right, pop_new = lax.optimization_barrier((left, right, pop_new))
    wide = jnp.concatenate([edge, left, right])
    above = send(wide, "gy", -1)
    below = send(wide, "gy", 1)
    devices = lax.axis_size("gx") * lax.axis_size("gy")
    levels, rows = call(
        levels_kernel,
        "levels",
        (f32(ITERS, 8, 8, 128), f32(devices, 128)),
        [(ITERS, 3, 10, 8, 128), (16, 128)],
        edge,
        left,
        right,
        above,
        below,
    )
    rows = lax.all_to_all(rows, ("gx", "gy"), 0, 0, tiled=True)
    (pot_new,) = call(combine_kernel, "combine", (f32(8, 8, 128),), [], rows, levels, kept[2])
    return (pop_new, conc_new, pot_new)


def solution(mesh):
    placed = (
        P(None, None, "gy", "gx"),
        P(None, None, "gy", "gx"),
        P(None, "gy", "gx"),
        P(None, "gy", "gx"),
        P(None, "gy", "gx"),
    )
    return jax.shard_map(
        local,
        mesh=mesh,
        in_specs=placed,
        out_specs=(P(None, None, "gy", "gx"), P(None, None, "gy", "gx"), P(None, "gy", "gx")),
        check_vma=False,
    )
```

```python
import jax
import jax.numpy as jnp
from jax import lax
from jax.experimental import pallas as pl
from jax.experimental.pallas import tpu as pltpu
from jax.sharding import PartitionSpec as P

STEPS = 4
ITERS = 8

lattice_velocity = (
    (0, 0, 0),
    (0, 0, 1),
    (0, 0, -1),
    (0, 1, 0),
    (0, -1, 0),
    (1, 0, 0),
    (-1, 0, 0),
    (0, 1, 1),
    (0, -1, -1),
    (0, 1, -1),
    (0, -1, 1),
    (1, 0, 1),
    (-1, 0, -1),
    (1, 0, -1),
    (-1, 0, 1),
    (1, 1, 0),
    (-1, -1, 0),
    (1, -1, 0),
    (-1, 1, 0),
)
opposite = (0, 2, 1, 4, 3, 6, 5, 8, 7, 10, 9, 12, 11, 14, 13, 16, 15, 18, 17)
lattice_weight = (1.0 / 3.0,) + (1.0 / 18.0,) * 6 + (1.0 / 36.0,) * 12
relax_time = 1.25
force_scale = 0.05
valences = (1.0, -1.0, 2.0)
diffusivity = (0.05, 0.07, 0.03)
diag_coef = 6.0001
surface_scale = 2.0

FIELDS = 25
XT = 7
YT = 97
F_CONC, F_FLUID, F_POT, F_POT2 = 19, 22, 23, 24
SLABS = 9
TILE = (8, 128)


def lane_id():
    return lax.broadcasted_iota(jnp.int32, TILE, 1)


def row_id():
    return lax.broadcasted_iota(jnp.int32, TILE, 0)


def rl(v, amount):
    amount = amount % 128
    return v if amount == 0 else pltpu.roll(v, amount, 1)


def rs(v, amount):
    amount = amount % 8
    return v if amount == 0 else pltpu.roll(v, amount, 0)


def in_lanes(lane, start, width):
    return (lane >= start) & (lane < start + width)


def pack_kernel(
    pop_in, conc_in, pot_in, solid_in, sign_in, pop, conc, pot, solid, sign,
    x_left, x_right, y_down, y_up, sems,
):
    lane, row = lane_id(), row_id()
    top = row < 4
    moves = []
    for i, (source, copy) in enumerate(
        ((pop_in, pop), (conc_in, conc), (pot_in, pot), (solid_in, solid), (sign_in, sign))
    ):
        moves.append(pltpu.make_async_copy(source, copy, sems.at[i]))
    for move in moves:
        move.start()
    for move in moves:
        move.wait()

    def tile(k, z):
        if k < F_CONC:
            return pop[k, z]
        if k < F_FLUID:
            return conc[k - F_CONC, z]
        if k == F_FLUID:
            return 1.0 - solid[z].astype(jnp.float32)
        return pot[z]

    for t in range(XT):
        left = right = jnp.zeros(TILE, jnp.float32)
        for q in range(4):
            k = 4 * t + q
            if k >= FIELDS:
                continue
            inner = 4 if k == F_POT2 else 0
            for z in range(8):
                v = tile(k, z)
                at = 16 * z + 4 * q
                here = in_lanes(lane, at, 4)
                left = jnp.where(here, rl(v, at - inner), left)
                right = jnp.where(here, rl(v, at - (124 - inner)), right)
            if k == F_POT2:
                low, high = tile(k, 0), tile(k, 0)
                low, high = rs(low, -4), rs(high, -3)
                for z in range(1, 8):
                    low = jnp.where(row == z, rs(tile(k, z), z - 4), low)
                    high = jnp.where(row == z, rs(tile(k, z), z - 3), high)
                y_down[4 * k] = low
                y_up[4 * k] = high
                continue
            for pair in range(4):
                a, b = tile(k, 2 * pair), tile(k, 2 * pair + 1)
                y_down[4 * k + pair] = jnp.where(top, a, rs(b, 4))
                y_up[4 * k + pair] = jnp.where(top, rs(a, 4), b)
        x_left[t] = left
        x_right[t] = right


def y_shift(a, b, cy, halves=(0, 1)):
    if cy == 0:
        return a, b
    edge = row_id() == (0 if cy > 0 else 7)
    ra, rb = rs(a, cy), rs(b, cy)
    return tuple(jnp.where(edge, rb, ra) if h == 0 else jnp.where(edge, ra, rb) for h in halves)


def x_shift(v, side, z, cx):
    if cx > 0:
        return jnp.where(lane_id() == 0, rl(side, -(16 * z + 3)), rl(v, 1))
    return jnp.where(lane_id() == 127, rl(side, 127 - (16 * z + 12)), rl(v, -1))


def shifted(get, offset, own=False):
    cz, cy, cx = offset
    halves = (0,) if own else (0, 1)
    side = y_shift(get(16), get(17), cy, halves) if cx or not own else None
    out = []
    for z in range(8):
        source = (z - cz) % 8
        v = y_shift(get(2 * source), get(2 * source + 1), cy, halves)
        if cx:
            v = tuple(x_shift(v[h], side[h], source, cx) for h in halves)
        out.append(v)
    if not own:
        out.append(tuple(rl(side[h], 16 * cz + cx) for h in halves))
    return out


def shifted_slab(get, offset, s):
    cz, cy, cx = offset
    if s == 8:
        v = y_shift(get(16), get(17), cy)
        return tuple(rl(x, 16 * cz + cx) for x in v)
    source = (s - cz) % 8
    v = y_shift(get(2 * source), get(2 * source + 1), cy)
    if cx:
        side = y_shift(get(16), get(17), cy)
        v = tuple(x_shift(v[h], side[h], source, cx) for h in range(2))
    return v


def step_kernel(
    pop, conc, pot, solid, sign, x_left, x_right, up, down, from_right, from_left, corner_up,
    corner_down, g, mask, cn, edge_out,
    f, below_rows, vel, cc, fluid, pt, dpot, field, flux,
):
    lane, row = lane_id(), row_id()
    top = row < 4
    slot = lane % 16

    def halves(k, z):
        u, d = up[4 * k + z // 2], down[4 * k + z // 2]
        if z % 2 == 0:
            return jnp.where(top, u, rs(d, 4))
        return jnp.where(top, rs(u, 4), d)

    def strip(k, tiles, low, high):
        q = k % 4
        out = jnp.where(slot < 4, rl(low, -4 * q), rl(high, 12 - 4 * q))
        for z in range(8):
            out = jnp.where(in_lanes(lane, 16 * z + 4, 4), rl(tiles[z], 16 * z + 4), out)
            out = jnp.where(in_lanes(lane, 16 * z + 8, 4), rl(tiles[z], 16 * z + 8 - 124), out)
        return out

    def strips(k, b):
        t = k // 4
        low = jnp.where(top, corner_up[XT + t], corner_down[XT + t])
        high = jnp.where(top, corner_up[t], corner_down[t])
        q = k % 4
        mine = jnp.where(
            slot < 8,
            jnp.where(slot < 4, rl(from_left[t], -4 * q), rl(x_left[t], 4 - 4 * q)),
            jnp.where(slot < 12, rl(x_right[t], 8 - 4 * q), rl(from_right[t], 12 - 4 * q)),
        )
        return mine, strip(k, b, low, high)

    def load(k, own, put):
        a = [own(z) for z in range(8)]
        b = [halves(k, z) for z in range(8)]
        for z in range(8):
            put(2 * z, a[z])
            put(2 * z + 1, b[z])
        sa, sb = strips(k, b)
        put(16, sa)
        put(17, sb)

    def putter(ref, *index):
        def put(i, v):
            ref[(*index, i)] = v

        return put

    for k in range(3):
        load(F_CONC + k, lambda z, k=k: conc[k, z], putter(cc, k))
    load(F_FLUID, lambda z: 1.0 - solid[z].astype(jnp.float32), putter(fluid))
    load(F_POT, lambda z: pot[z], putter(pt))

    for i in range(1, 19):
        moved = shifted(lambda s: fluid[s], lattice_velocity[i])
        for s in range(SLABS):
            for h in range(2):
                mask[i - 1, 2 * s + h] = moved[s][h] * fluid[2 * s + h]

    u, d = up[4 * F_POT2], down[4 * F_POT2]
    far = [jnp.where(row == 3, rs(u, 3 - z), rs(d, 4 - z)) for z in range(8)]
    t2, q2 = F_POT2 // 4, F_POT2 % 4
    tp = F_POT // 4
    far_low = jnp.where(row == 3, rs(corner_up[XT + tp], -1), rs(corner_down[XT + tp], 1))
    far_high = jnp.where(row == 3, rs(corner_up[tp], -1), rs(corner_down[tp], 1))
    far.append(strip(F_POT, far, far_low, far_high))
    edge_low = (from_left[t2], jnp.where(top, corner_up[XT + t2], corner_down[XT + t2]))
    edge_high = (from_right[t2], jnp.where(top, corner_up[t2], corner_down[t2]))
    for axis in range(3):
        plus = tuple(1 if d == axis else 0 for d in range(3))
        minus = tuple(-p for p in plus)
        below = shifted(lambda s: pt[s], plus)
        above = shifted(lambda s: pt[s], minus)
        for s in range(SLABS):
            for h in range(2):
                lo, hi = below[s][h], above[s][h]
                if axis == 1 and h == 1:
                    lo = jnp.where(row == 4, far[s], lo)
                    hi = jnp.where(row == 3, far[s], hi)
                if axis == 2 and s == 8:
                    lo = jnp.where(slot == 0, rl(edge_low[h], -4 * q2 - 3), lo)
                    hi = jnp.where(slot == 15, rl(edge_high[h], 15 - 4 * q2), hi)
                    for z in range(8):
                        hi = jnp.where(lane == 16 * z + 7, rl(pt[2 * z + h], 16 * z + 3), hi)
                here = pt[2 * s + h]
                if h == 0 and s < 8:
                    dpot[3 + axis, 2 * s] = here - lo
                dpot[axis, 2 * s + h] = hi - here
                field[axis, 2 * s + h] = (0.5 * force_scale) * (lo - hi)

    pairs = [(i, i + 1) for i in range(1, 19, 2)]

    def along(c, vector):
        running = None
        for d in range(3):
            if c[d] != 0:
                if running is None:
                    running = vector[d] if c[d] > 0 else -vector[d]
                else:
                    running = running + vector[d] if c[d] > 0 else running - vector[d]
        return running

    def collide(s, v):
        total = {}
        delta = {}
        for a, b in pairs:
            total[a] = v[a] + v[b]
            delta[a] = v[a] - v[b]
        density = (
            v[0]
            + ((total[1] + total[3]) + (total[5] + total[7]))
            + ((total[9] + total[11]) + (total[13] + total[15]) + total[17])
        )
        momentum = (
            (delta[5] + delta[11]) + (delta[13] + delta[15]) + delta[17],
            (delta[3] + delta[7]) + (delta[9] + delta[15]) - delta[17],
            (delta[1] + delta[7]) - (delta[9] - delta[11]) - delta[13],
        )
        open_cell = fluid[s]
        charge = open_cell * (
            valences[0] * cc[0, s] + valences[1] * cc[1, s] + valences[2] * cc[2, s]
        )
        force = [charge * field[d, s] for d in range(3)]
        inverse = 1.0 / density
        u = [(momentum[d] + 0.5 * force[d]) * inverse for d in range(3)]
        for d in range(3):
            vel[d, s] = u[d]
        speed = u[0] * u[0] + u[1] * u[1] + u[2] * u[2]
        work = u[0] * force[0] + u[1] * force[1] + u[2] * force[2]
        flow = [density * u[d] for d in range(3)]
        keep = 1.0 - 1.0 / relax_time
        gain = 1.0 / relax_time
        push = 1.0 - 0.5 / relax_time
        base = gain * density - (1.5 * gain) * (density * speed) - (3.0 * push) * work
        odd = [(3.0 * gain) * flow[d] + (3.0 * push) * force[d] for d in range(3)]
        even = [(4.5 * gain) * flow[d] + (9.0 * push) * force[d] for d in range(3)]
        is_open = open_cell > 0.5
        g[0, s] = jnp.where(is_open, keep * v[0] + lattice_weight[0] * base, v[0])
        for a, b in pairs:
            c, w = lattice_velocity[a], lattice_weight[a]
            middle = base + along(c, u) * along(c, even)
            side = along(c, odd)
            g[a, s] = jnp.where(is_open, keep * v[a] + w * (middle + side), v[b])
            g[b, s] = jnp.where(is_open, keep * v[b] + w * (middle - side), v[a])

    for z in range(8):
        collide(2 * z, [pop[k, z] for k in range(19)])
    for z in range(8):
        v = [halves(k, z) for k in range(19)]
        for k in range(19):
            below_rows[k, z] = v[k]
        collide(2 * z + 1, v)
    both = [
        strips(k, [below_rows[k, z] for z in range(8)])
        for k in range(19)
    ]
    for h in range(2):
        collide(16 + h, [both[k][h] for k in range(19)])

    def stream():
        for s in range(2 * SLABS):
            f[0, s] = g[0, s]
        for s in range(SLABS):
            for i in range(1, 19):
                moved = shifted_slab(lambda n, i=i: g[i, n], lattice_velocity[i], s)
                for h in range(2):
                    n = 2 * s + h
                    f[i, n] = jnp.where(mask[i - 1, n] > 0.5, moved[h], g[opposite[i], n])
        for s in range(2 * SLABS):
            collide(s, [f[i, s] for i in range(19)])

    def ions(own=False):
        for axis in range(3):
            plus = tuple(1 if d == axis else 0 for d in range(3))
            minus = tuple(-p for p in plus)
            upper = 2 * (2 - axis) + 1
            for s in [8] + list(range(8)):
                v_high = shifted_slab(lambda n: vel[axis, n], minus, s)
                c_high = [shifted_slab(lambda n, k=k: cc[k, n], minus, s) for k in range(3)]
                for h in range(2):
                    n = 2 * s + h
                    speed = 0.25 * (vel[axis, n] + v_high[h])
                    step, is_open = dpot[axis, n], mask[upper, n]
                    for k in range(3):
                        rate = diffusivity[k]
                        here, hi = cc[k, n], c_high[k][h]
                        pull = speed - (0.5 * rate * valences[k]) * step
                        flux[axis, k, n] = is_open * (rate * (here - hi) + (here + hi) * pull)
        for k in range(3):
            for s in range(8 if own else SLABS):
                low = [
                    shifted_slab(
                        lambda n, d=d: flux[d, k, n], tuple(1 if e == d else 0 for e in range(3)), s
                    )
                    for d in range(3)
                ]
                for h in range(1 if own else 2):
                    n = 2 * s + h
                    net = [flux[d, k, n] - low[d][h] for d in range(3)]
                    cn[k, n] = cc[k, n] - ((net[0] + net[1]) + net[2])

    def one_step(step, carry):
        ions()
        for k in range(3):
            for n in range(2 * SLABS):
                cc[k, n] = cn[k, n]
        stream()
        return carry

    lax.fori_loop(0, STEPS - 1, one_step, 0)
    ions(own=True)

    edge = jnp.zeros(TILE, jnp.float32)
    for z in range(8):
        n = 2 * z
        c = [cn[k, n] for k in range(3)]
        open_cell = fluid[n]
        target = open_cell * (
            valences[0] * c[0] + valences[1] * c[1] + valences[2] * c[2]
        ) + surface_scale * sign[z].astype(jnp.float32) * (1.0 - open_cell)
        spread = (
            (dpot[0, n] - dpot[3, n]) + (dpot[1, n] - dpot[4, n]) + (dpot[2, n] - dpot[5, n])
        )
        residual = target - ((diag_coef - 6.0) * pt[n] - spread)
        edge_out[z] = residual
        edge = jnp.where(in_lanes(lane, 16 * z, 8), rl(residual, 16 * z - 120), edge)
        edge = jnp.where(in_lanes(lane, 16 * z + 8, 8), rl(residual, 16 * z + 8), edge)
    edge_out[8] = edge


STEP_SHAPES = (
    (
        (19, 2 * SLABS, 8, 128),
        (18, 2 * SLABS, 8, 128),
        (3, 2 * SLABS, 8, 128),
        (9, 8, 128),
    ),
    (
        (19, 2 * SLABS, 8, 128),
        (19, 8, 8, 128),
        (3, 2 * SLABS, 8, 128),
        (3, 2 * SLABS, 8, 128),
        (2 * SLABS, 8, 128),
        (2 * SLABS, 8, 128),
        (6, 2 * SLABS, 8, 128),
        (3, 2 * SLABS, 8, 128),
        (3, 3, 2 * SLABS, 8, 128),
    ),
)


def finish_kernel(g, mask, conc, pop_out, conc_out):
    for z in range(8):
        for k in range(3):
            conc_out[k, z] = conc[k, 2 * z]
        pop_out[0, z] = g[0, 2 * z]
    for i in range(1, 19):
        moved = shifted(lambda s, i=i: g[i, s], lattice_velocity[i], own=True)
        for z in range(8):
            pop_out[i, z] = jnp.where(
                mask[i - 1, 2 * z] > 0.5, moved[z][0], g[opposite[i], 2 * z]
            )


def levels_kernel(own, left, right, up, down, level_out, row_out, lv, part):
    lane, row = lane_id(), row_id()
    slot = lane % 16
    first_row, last_row = row == 0, row == 7
    first_lane, last_lane = lane == 0, lane == 127
    sources = (
        (own, left[0], right[0]),
        (up, up[9], up[10]),
        (down, down[9], down[10]),
    )
    for r, (main, low, high) in enumerate(sources):
        for s in range(8):
            lv[0, r, s] = main[s]
        lv[0, r, 8] = jnp.where(slot < 8, low, main[8])
        lv[0, r, 9] = jnp.where(slot < 8, main[8], high)

    def around(j, r, s, low, high):
        v = lv[j, r, s]
        above, below = lv[j, (r + 1) % 3, s], lv[j, (r + 2) % 3, s]
        vertical = jnp.where(last_row, rs(above, -1), rs(v, -1)) + jnp.where(
            first_row, rs(below, 1), rs(v, 1)
        )
        if s < 8:
            across = jnp.where(first_lane, rl(low, -(16 * s + 7)), rl(v, 1)) + jnp.where(
                last_lane, rl(high, 127 - (16 * s + 8)), rl(v, -1)
            )
            return (lv[j, r, (s + 1) % 8] + lv[j, r, (s - 1) % 8]) + vertical + across
        return (rl(v, 16) + rl(v, -16)) + vertical + (rl(v, 1) + rl(v, -1))

    for j in range(ITERS):
        done = j == ITERS - 1
        squares = products = jnp.zeros(TILE, jnp.float32)
        for r in range(1 if done else 3):
            low, high = lv[j, r, 8], lv[j, r, 9]
            for s in range(8 if done else 10):
                total = around(j, r, s, low, high)
                if j == 0:
                    fresh = -total / 6.0
                else:
                    fresh = total * (-1.0 / 3.0) - lv[j - 1, r, s]
                if not done:
                    lv[j + 1, r, s] = fresh
                if r == 0 and s < 8:
                    here = lv[j, 0, s]
                    level_out[j, s] = here
                    squares = squares + here * here
                    products = products + here * fresh
        part[j : j + 1, :] = jnp.sum(squares, axis=0, keepdims=True)
        part[8 + j : 9 + j, :] = jnp.sum(products, axis=0, keepdims=True)
    sums = jnp.sum(part[...], axis=1, keepdims=True)
    diagonal = lax.broadcasted_iota(jnp.int32, (16, 128), 0) == lax.broadcasted_iota(
        jnp.int32, (16, 128), 1
    )
    one_row = jnp.sum(jnp.where(diagonal, sums, 0.0), axis=0, keepdims=True)
    row_out[...] = jnp.broadcast_to(one_row, row_out.shape)


def combine_kernel(rows, levels, pot, out):
    total = jnp.broadcast_to(jnp.sum(rows[...], axis=0, keepdims=True), (16, 128))
    diagonal = lax.broadcasted_iota(jnp.int32, (16, 128), 0) == lax.broadcasted_iota(
        jnp.int32, (16, 128), 1
    )
    sums = jnp.sum(jnp.where(diagonal, total, 0.0), axis=1, keepdims=True)

    def entry(i):
        return jnp.broadcast_to(sums[i : i + 1, :], TILE)

    moment = [None] * 16
    moment[0], moment[1] = entry(0), entry(8)
    for k in range(1, ITERS):
        moment[2 * k] = 2.0 * entry(k) - moment[0]
        moment[2 * k + 1] = 2.0 * entry(8 + k) - moment[1]
    gram = {}
    for i in range(ITERS + 1):
        for j in range(i, ITERS + 1):
            if i + j < 16:
                gram[i, j] = gram[j, i] = 0.5 * (moment[i + j] + moment[j - i])

    def add_up(terms):
        while len(terms) > 1:
            terms = [
                terms[i] + terms[i + 1] if i + 1 < len(terms) else terms[i]
                for i in range(0, len(terms), 2)
            ]
        return terms[0]

    def inner(a, b):
        return add_up(
            [x * add_up([gram[i, j] * y for j, y in enumerate(b)]) for i, x in enumerate(a)]
        )

    one, zero = jnp.ones(TILE, jnp.float32), jnp.zeros(TILE, jnp.float32)
    search, rest, found = [one], [one], []
    left = moment[0]
    for k in range(ITERS):
        image = [zero] * (k + 2)
        for j in range(k + 1):
            image[j] = image[j] + diag_coef * search[j]
            if j == 0:
                image[1] = image[1] + 6.0 * search[0]
            else:
                image[j + 1] = image[j + 1] + 3.0 * search[j]
                image[j - 1] = image[j - 1] + 3.0 * search[j]
        length = left / inner(search, image)
        found = [
            (found[j] if j < len(found) else zero) + length * search[j] for j in range(k + 1)
        ]
        if k == ITERS - 1:
            break
        rest = [(rest[j] if j < k + 1 else zero) - length * image[j] for j in range(k + 2)]
        fresh = inner(rest, rest)
        ratio = fresh / left
        search = [rest[j] + (ratio * search[j] if j < k + 1 else zero) for j in range(k + 2)]
        left = fresh
    for z in range(8):
        running = found[0] * levels[0, z]
        for j in range(1, ITERS):
            running = running + found[j] * levels[j, z]
        out[z] = pot[z] + running


def in_vmem(count):
    return [pl.BlockSpec(memory_space=pltpu.VMEM)] * count


def f32(*shape):
    return jax.ShapeDtypeStruct(shape, jnp.float32)


def call(kernel, name, outs, scratch, *args, in_specs=None):
    return pl.pallas_call(
        kernel,
        name=name,
        out_shape=outs,
        in_specs=in_specs or in_vmem(len(args)),
        out_specs=in_vmem(len(outs)),
        scratch_shapes=[
            pltpu.VMEM(shape, jnp.float32) if isinstance(shape, tuple) else shape
            for shape in scratch
        ],
        compiler_params=pltpu.CompilerParams(vmem_limit_bytes=48 << 20),
    )(*args)


def send(block, axis, step):
    count = lax.axis_size(axis)
    return lax.ppermute(block, axis, [(i, (i + step) % count) for i in range(count)])


def local(populations, concentrations, potential, solid_mask, surface_sign):
    inputs = tuple(
        pltpu.with_memory_space_constraint(a, pltpu.HBM)
        for a in (populations, concentrations, potential, solid_mask, surface_sign)
    )
    packed = call(
        pack_kernel,
        "pack",
        tuple(jax.ShapeDtypeStruct(a.shape, a.dtype) for a in inputs)
        + (f32(XT, 8, 128), f32(XT, 8, 128), f32(YT, 8, 128), f32(YT, 8, 128)),
        [pltpu.SemaphoreType.DMA((5,))],
        *inputs,
        in_specs=[pl.BlockSpec(memory_space=pltpu.HBM)] * 5,
    )
    kept, (x_left, x_right, y_down, y_up) = packed[:5], packed[5:]
    up = send(y_down, "gy", -1)
    down = send(y_up, "gy", 1)
    from_right = send(x_left, "gx", -1)
    from_left = send(x_right, "gx", 1)
    corner = jnp.concatenate([from_right, from_left])
    corner_up = send(corner, "gy", -1)
    corner_down = send(corner, "gy", 1)
    relaxed, mask, conc_last, edge = call(
        step_kernel,
        "steps",
        tuple(f32(*shape) for shape in STEP_SHAPES[0]),
        STEP_SHAPES[1],
        *kept,
        x_left,
        x_right,
        up,
        down,
        from_right,
        from_left,
        corner_up,
        corner_down,
    )
    strip = edge[8:]
    left = send(strip, "gx", 1)
    right = send(strip, "gx", -1)
    pop_new, conc_new = call(
        finish_kernel,
        "finish",
        (f32(19, 8, 8, 128), f32(3, 8, 8, 128)),
        [],
        relaxed,
        mask,
        conc_last,
    )
    left, right, pop_new, conc_new = lax.optimization_barrier((left, right, pop_new, conc_new))
    wide = jnp.concatenate([edge, left, right])
    above = send(wide, "gy", -1)
    below = send(wide, "gy", 1)
    devices = lax.axis_size("gx") * lax.axis_size("gy")
    levels, rows = call(
        levels_kernel,
        "levels",
        (f32(ITERS, 8, 8, 128), f32(devices, 128)),
        [(ITERS, 3, 10, 8, 128), (16, 128)],
        edge,
        left,
        right,
        above,
        below,
    )
    rows = lax.all_to_all(rows, ("gx", "gy"), 0, 0, tiled=True)
    (pot_new,) = call(combine_kernel, "combine", (f32(8, 8, 128),), [], rows, levels, kept[2])
    return (pop_new, conc_new, pot_new)


def solution(mesh):
    placed = (
        P(None, None, "gy", "gx"),
        P(None, None, "gy", "gx"),
        P(None, "gy", "gx"),
        P(None, "gy", "gx"),
        P(None, "gy", "gx"),
    )
    return jax.shard_map(
        local,
        mesh=mesh,
        in_specs=placed,
        out_specs=(P(None, None, "gy", "gx"), P(None, None, "gy", "gx"), P(None, "gy", "gx")),
        check_vma=False,
    )
```

```python
import jax
import jax.numpy as jnp
from jax import lax
from jax.experimental import pallas as pl
from jax.experimental.pallas import tpu as pltpu
from jax.sharding import PartitionSpec as P

STEPS = 4
ITERS = 8

lattice_velocity = (
    (0, 0, 0),
    (0, 0, 1),
    (0, 0, -1),
    (0, 1, 0),
    (0, -1, 0),
    (1, 0, 0),
    (-1, 0, 0),
    (0, 1, 1),
    (0, -1, -1),
    (0, 1, -1),
    (0, -1, 1),
    (1, 0, 1),
    (-1, 0, -1),
    (1, 0, -1),
    (-1, 0, 1),
    (1, 1, 0),
    (-1, -1, 0),
    (1, -1, 0),
    (-1, 1, 0),
)
opposite = (0, 2, 1, 4, 3, 6, 5, 8, 7, 10, 9, 12, 11, 14, 13, 16, 15, 18, 17)
lattice_weight = (1.0 / 3.0,) + (1.0 / 18.0,) * 6 + (1.0 / 36.0,) * 12
relax_time = 1.25
force_scale = 0.05
valences = (1.0, -1.0, 2.0)
diffusivity = (0.05, 0.07, 0.03)
diag_coef = 6.0001
surface_scale = 2.0

FIELDS = 25
XT = 7
YT = 97
F_CONC, F_FLUID, F_POT, F_POT2 = 19, 22, 23, 24
SLABS = 9
TILE = (8, 128)


def lane_id():
    return lax.broadcasted_iota(jnp.int32, TILE, 1)


def row_id():
    return lax.broadcasted_iota(jnp.int32, TILE, 0)


def rl(v, amount):
    amount = amount % 128
    return v if amount == 0 else pltpu.roll(v, amount, 1)


def rs(v, amount):
    amount = amount % 8
    return v if amount == 0 else pltpu.roll(v, amount, 0)


def in_lanes(lane, start, width):
    return (lane >= start) & (lane < start + width)


def pack_kernel(
    pop_in, conc_in, pot_in, solid_in, sign_in, pop, conc, pot, solid, sign,
    x_left, x_right, y_down, y_up, sems,
):
    lane, row = lane_id(), row_id()
    top = row < 4
    moves = []
    for i, (source, copy) in enumerate(
        ((pop_in, pop), (conc_in, conc), (pot_in, pot), (solid_in, solid), (sign_in, sign))
    ):
        moves.append(pltpu.make_async_copy(source, copy, sems.at[i]))
    for move in moves:
        move.start()
    for move in moves:
        move.wait()

    def tile(k, z):
        if k < F_CONC:
            return pop[k, z]
        if k < F_FLUID:
            return conc[k - F_CONC, z]
        if k == F_FLUID:
            return 1.0 - solid[z].astype(jnp.float32)
        return pot[z]

    for t in range(XT):
        left = right = jnp.zeros(TILE, jnp.float32)
        for q in range(4):
            k = 4 * t + q
            if k >= FIELDS:
                continue
            inner = 4 if k == F_POT2 else 0
            for z in range(8):
                v = tile(k, z)
                at = 16 * z + 4 * q
                here = in_lanes(lane, at, 4)
                left = jnp.where(here, rl(v, at - inner), left)
                right = jnp.where(here, rl(v, at - (124 - inner)), right)
            if k == F_POT2:
                low, high = tile(k, 0), tile(k, 0)
                low, high = rs(low, -4), rs(high, -3)
                for z in range(1, 8):
                    low = jnp.where(row == z, rs(tile(k, z), z - 4), low)
                    high = jnp.where(row == z, rs(tile(k, z), z - 3), high)
                y_down[4 * k] = low
                y_up[4 * k] = high
                continue
            for pair in range(4):
                a, b = tile(k, 2 * pair), tile(k, 2 * pair + 1)
                y_down[4 * k + pair] = jnp.where(top, a, rs(b, 4))
                y_up[4 * k + pair] = jnp.where(top, rs(a, 4), b)
        x_left[t] = left
        x_right[t] = right


def corner_kernel(right, left, down_out, up_out):
    top = row_id() < 4
    for t in range(XT):
        a, b = right[t], rs(left[t], 4)
        down_out[t] = jnp.where(top, a, b)
        up_out[t] = jnp.where(top, b, a)
    tp = F_POT // 4
    a, b = rs(right[tp], 4), left[tp]
    down_out[XT] = jnp.where(top, a, b)
    up_out[XT] = jnp.where(top, b, a)


def y_shift(a, b, cy, halves=(0, 1)):
    if cy == 0:
        return a, b
    edge = row_id() == (0 if cy > 0 else 7)
    ra, rb = rs(a, cy), rs(b, cy)
    return tuple(jnp.where(edge, rb, ra) if h == 0 else jnp.where(edge, ra, rb) for h in halves)


def x_shift(v, side, z, cx):
    if cx > 0:
        return jnp.where(lane_id() == 0, rl(side, -(16 * z + 3)), rl(v, 1))
    return jnp.where(lane_id() == 127, rl(side, 127 - (16 * z + 12)), rl(v, -1))


def shifted(get, offset, own=False):
    cz, cy, cx = offset
    halves = (0,) if own else (0, 1)
    side = y_shift(get(16), get(17), cy, halves) if cx or not own else None
    out = []
    for z in range(8):
        source = (z - cz) % 8
        v = y_shift(get(2 * source), get(2 * source + 1), cy, halves)
        if cx:
            v = tuple(x_shift(v[h], side[h], source, cx) for h in halves)
        out.append(v)
    if not own:
        out.append(tuple(rl(side[h], 16 * cz + cx) for h in halves))
    return out


def shifted_slab(get, offset, s):
    cz, cy, cx = offset
    if s == 8:
        v = y_shift(get(16), get(17), cy)
        return tuple(rl(x, 16 * cz + cx) for x in v)
    source = (s - cz) % 8
    v = y_shift(get(2 * source), get(2 * source + 1), cy)
    if cx:
        side = y_shift(get(16), get(17), cy)
        v = tuple(x_shift(v[h], side[h], source, cx) for h in range(2))
    return v


def step_kernel(
    pop, conc, pot, solid, sign, x_left, x_right, down, up, from_right, from_left, corner_up,
    corner_down, g, mask, cn, edge_out,
    f, below_rows, vel, cc, fluid, pt, dpot, field, flux,
):
    lane, row = lane_id(), row_id()
    top = row < 4
    slot = lane % 16

    def halves(k, z):
        u, d = up[4 * k + z // 2], down[4 * k + z // 2]
        if z % 2 == 0:
            return jnp.where(top, u, rs(d, 4))
        return jnp.where(top, rs(u, 4), d)

    def strip(k, tiles, low, high):
        q = k % 4
        out = jnp.where(slot < 4, rl(low, -4 * q), rl(high, 12 - 4 * q))
        for z in range(8):
            out = jnp.where(in_lanes(lane, 16 * z + 4, 4), rl(tiles[z], 16 * z + 4), out)
            out = jnp.where(in_lanes(lane, 16 * z + 8, 4), rl(tiles[z], 16 * z + 8 - 124), out)
        return out

    def corners(t):
        u, d = corner_up[t], corner_down[t]
        return rs(jnp.where(top, d, u), 4), jnp.where(top, u, d)

    def strips(k, b):
        t = k // 4
        low, high = corners(t)
        q = k % 4
        mine = jnp.where(
            slot < 8,
            jnp.where(slot < 4, rl(from_left[t], -4 * q), rl(x_left[t], 4 - 4 * q)),
            jnp.where(slot < 12, rl(x_right[t], 8 - 4 * q), rl(from_right[t], 12 - 4 * q)),
        )
        return mine, strip(k, b, low, high)

    def load(k, own, put):
        a = [own(z) for z in range(8)]
        b = [halves(k, z) for z in range(8)]
        for z in range(8):
            put(2 * z, a[z])
            put(2 * z + 1, b[z])
        sa, sb = strips(k, b)
        put(16, sa)
        put(17, sb)

    def putter(ref, *index):
        def put(i, v):
            ref[(*index, i)] = v

        return put

    for k in range(3):
        load(F_CONC + k, lambda z, k=k: conc[k, z], putter(cc, k))
    load(F_FLUID, lambda z: 1.0 - solid[z].astype(jnp.float32), putter(fluid))
    load(F_POT, lambda z: pot[z], putter(pt))

    for i in range(1, 19):
        moved = shifted(lambda s: fluid[s], lattice_velocity[i])
        for s in range(SLABS):
            for h in range(2):
                mask[i - 1, 2 * s + h] = moved[s][h] * fluid[2 * s + h]

    u, d = up[4 * F_POT2], down[4 * F_POT2]
    far = [jnp.where(row == 3, rs(u, 3 - z), rs(d, 4 - z)) for z in range(8)]
    t2, q2 = F_POT2 // 4, F_POT2 % 4
    u, d = corner_up[XT], corner_down[XT]
    far_low = jnp.where(row == 3, rs(u, -1), rs(d, 1))
    far_high = jnp.where(row == 3, rs(u, 3), rs(d, -3))
    far.append(strip(F_POT, far, far_low, far_high))
    low, high = corners(t2)
    edge_low, edge_high = (from_left[t2], low), (from_right[t2], high)
    for axis in range(3):
        plus = tuple(1 if d == axis else 0 for d in range(3))
        minus = tuple(-p for p in plus)
        below = shifted(lambda s: pt[s], plus)
        above = shifted(lambda s: pt[s], minus)
        for s in range(SLABS):
            for h in range(2):
                lo, hi = below[s][h], above[s][h]
                if axis == 1 and h == 1:
                    lo = jnp.where(row == 4, far[s], lo)
                    hi = jnp.where(row == 3, far[s], hi)
                if axis == 2 and s == 8:
                    lo = jnp.where(slot == 0, rl(edge_low[h], -4 * q2 - 3), lo)
                    hi = jnp.where(slot == 15, rl(edge_high[h], 15 - 4 * q2), hi)
                    for z in range(8):
                        hi = jnp.where(lane == 16 * z + 7, rl(pt[2 * z + h], 16 * z + 3), hi)
                here = pt[2 * s + h]
                if h == 0 and s < 8:
                    dpot[3 + axis, 2 * s] = here - lo
                dpot[axis, 2 * s + h] = hi - here
                field[axis, 2 * s + h] = (0.5 * force_scale) * (lo - hi)

    pairs = [(i, i + 1) for i in range(1, 19, 2)]

    def along(c, vector):
        running = None
        for d in range(3):
            if c[d] != 0:
                if running is None:
                    running = vector[d] if c[d] > 0 else -vector[d]
                else:
                    running = running + vector[d] if c[d] > 0 else running - vector[d]
        return running

    def collide(s, v):
        total = {}
        delta = {}
        for a, b in pairs:
            total[a] = v[a] + v[b]
            delta[a] = v[a] - v[b]
        density = (
            v[0]
            + ((total[1] + total[3]) + (total[5] + total[7]))
            + ((total[9] + total[11]) + (total[13] + total[15]) + total[17])
        )
        momentum = (
            (delta[5] + delta[11]) + (delta[13] + delta[15]) + delta[17],
            (delta[3] + delta[7]) + (delta[9] + delta[15]) - delta[17],
            (delta[1] + delta[7]) - (delta[9] - delta[11]) - delta[13],
        )
        open_cell = fluid[s]
        charge = open_cell * (
            valences[0] * cc[0, s] + valences[1] * cc[1, s] + valences[2] * cc[2, s]
        )
        force = [charge * field[d, s] for d in range(3)]
        inverse = 1.0 / density
        u = [(momentum[d] + 0.5 * force[d]) * inverse for d in range(3)]
        for d in range(3):
            vel[d, s] = u[d]
        speed = u[0] * u[0] + u[1] * u[1] + u[2] * u[2]
        work = u[0] * force[0] + u[1] * force[1] + u[2] * force[2]
        flow = [density * u[d] for d in range(3)]
        keep = 1.0 - 1.0 / relax_time
        gain = 1.0 / relax_time
        push = 1.0 - 0.5 / relax_time
        base = gain * density - (1.5 * gain) * (density * speed) - (3.0 * push) * work
        odd = [(3.0 * gain) * flow[d] + (3.0 * push) * force[d] for d in range(3)]
        even = [(4.5 * gain) * flow[d] + (9.0 * push) * force[d] for d in range(3)]
        is_open = open_cell > 0.5
        g[0, s] = jnp.where(is_open, keep * v[0] + lattice_weight[0] * base, v[0])
        for a, b in pairs:
            c, w = lattice_velocity[a], lattice_weight[a]
            middle = base + along(c, u) * along(c, even)
            side = along(c, odd)
            g[a, s] = jnp.where(is_open, keep * v[a] + w * (middle + side), v[b])
            g[b, s] = jnp.where(is_open, keep * v[b] + w * (middle - side), v[a])

    for z in range(8):
        collide(2 * z, [pop[k, z] for k in range(19)])
    for z in range(8):
        v = [halves(k, z) for k in range(19)]
        for k in range(19):
            below_rows[k, z] = v[k]
        collide(2 * z + 1, v)
    both = [
        strips(k, [below_rows[k, z] for z in range(8)])
        for k in range(19)
    ]
    for h in range(2):
        collide(16 + h, [both[k][h] for k in range(19)])

    def stream():
        for s in range(2 * SLABS):
            f[0, s] = g[0, s]
        for s in range(SLABS):
            for i in range(1, 19):
                moved = shifted_slab(lambda n, i=i: g[i, n], lattice_velocity[i], s)
                for h in range(2):
                    n = 2 * s + h
                    f[i, n] = jnp.where(mask[i - 1, n] > 0.5, moved[h], g[opposite[i], n])
        for s in range(2 * SLABS):
            collide(s, [f[i, s] for i in range(19)])

    def ions(own=False):
        for axis in range(3):
            plus = tuple(1 if d == axis else 0 for d in range(3))
            minus = tuple(-p for p in plus)
            upper = 2 * (2 - axis) + 1
            for s in [8] + list(range(8)):
                v_high = shifted_slab(lambda n: vel[axis, n], minus, s)
                c_high = [shifted_slab(lambda n, k=k: cc[k, n], minus, s) for k in range(3)]
                for h in range(2):
                    n = 2 * s + h
                    speed = 0.25 * (vel[axis, n] + v_high[h])
                    step, is_open = dpot[axis, n], mask[upper, n]
                    for k in range(3):
                        rate = diffusivity[k]
                        here, hi = cc[k, n], c_high[k][h]
                        pull = speed - (0.5 * rate * valences[k]) * step
                        flux[axis, k, n] = is_open * (rate * (here - hi) + (here + hi) * pull)
        for k in range(3):
            for s in range(8 if own else SLABS):
                low = [
                    shifted_slab(
                        lambda n, d=d: flux[d, k, n], tuple(1 if e == d else 0 for e in range(3)), s
                    )
                    for d in range(3)
                ]
                for h in range(1 if own else 2):
                    n = 2 * s + h
                    net = [flux[d, k, n] - low[d][h] for d in range(3)]
                    cn[k, n] = cc[k, n] - ((net[0] + net[1]) + net[2])

    def one_step(step, carry):
        ions()
        for k in range(3):
            for n in range(2 * SLABS):
                cc[k, n] = cn[k, n]
        stream()
        return carry

    lax.fori_loop(0, STEPS - 1, one_step, 0)
    ions(own=True)

    edge = jnp.zeros(TILE, jnp.float32)
    for z in range(8):
        n = 2 * z
        c = [cn[k, n] for k in range(3)]
        open_cell = fluid[n]
        target = open_cell * (
            valences[0] * c[0] + valences[1] * c[1] + valences[2] * c[2]
        ) + surface_scale * sign[z].astype(jnp.float32) * (1.0 - open_cell)
        spread = (
            (dpot[0, n] - dpot[3, n]) + (dpot[1, n] - dpot[4, n]) + (dpot[2, n] - dpot[5, n])
        )
        residual = target - ((diag_coef - 6.0) * pt[n] - spread)
        edge_out[z] = residual
        edge = jnp.where(in_lanes(lane, 16 * z, 8), rl(residual, 16 * z - 120), edge)
        edge = jnp.where(in_lanes(lane, 16 * z + 8, 8), rl(residual, 16 * z + 8), edge)
    edge_out[8] = edge


STEP_SHAPES = (
    (
        (19, 2 * SLABS, 8, 128),
        (18, 2 * SLABS, 8, 128),
        (3, 2 * SLABS, 8, 128),
        (9, 8, 128),
    ),
    (
        (19, 2 * SLABS, 8, 128),
        (19, 8, 8, 128),
        (3, 2 * SLABS, 8, 128),
        (3, 2 * SLABS, 8, 128),
        (2 * SLABS, 8, 128),
        (2 * SLABS, 8, 128),
        (6, 2 * SLABS, 8, 128),
        (3, 2 * SLABS, 8, 128),
        (3, 3, 2 * SLABS, 8, 128),
    ),
)


def finish_kernel(g, mask, conc, pop_out, conc_out):
    for z in range(8):
        for k in range(3):
            conc_out[k, z] = conc[k, 2 * z]
        pop_out[0, z] = g[0, 2 * z]
    for i in range(1, 19):
        moved = shifted(lambda s, i=i: g[i, s], lattice_velocity[i], own=True)
        for z in range(8):
            pop_out[i, z] = jnp.where(
                mask[i - 1, 2 * z] > 0.5, moved[z][0], g[opposite[i], 2 * z]
            )


def levels_kernel(own, left, right, down, up, level_out, row_out, lv, part):
    lane, row = lane_id(), row_id()
    slot = lane % 16
    first_row, last_row = row == 0, row == 7
    first_lane, last_lane = lane == 0, lane == 127
    sources = (
        (own, left[0], right[0]),
        (up, up[9], up[10]),
        (down, down[9], down[10]),
    )
    for r, (main, low, high) in enumerate(sources):
        for s in range(8):
            lv[0, r, s] = main[s]
        lv[0, r, 8] = jnp.where(slot < 8, low, main[8])
        lv[0, r, 9] = jnp.where(slot < 8, main[8], high)

    def around(j, r, s, low, high):
        v = lv[j, r, s]
        above, below = lv[j, (r + 1) % 3, s], lv[j, (r + 2) % 3, s]
        vertical = jnp.where(last_row, rs(above, -1), rs(v, -1)) + jnp.where(
            first_row, rs(below, 1), rs(v, 1)
        )
        if s < 8:
            across = jnp.where(first_lane, rl(low, -(16 * s + 7)), rl(v, 1)) + jnp.where(
                last_lane, rl(high, 127 - (16 * s + 8)), rl(v, -1)
            )
            return (lv[j, r, (s + 1) % 8] + lv[j, r, (s - 1) % 8]) + vertical + across
        return (rl(v, 16) + rl(v, -16)) + vertical + (rl(v, 1) + rl(v, -1))

    for j in range(ITERS):
        done = j == ITERS - 1
        squares = products = jnp.zeros(TILE, jnp.float32)
        for r in range(1 if done else 3):
            low, high = lv[j, r, 8], lv[j, r, 9]
            for s in range(8 if done else 10):
                total = around(j, r, s, low, high)
                if j == 0:
                    fresh = -total / 6.0
                else:
                    fresh = total * (-1.0 / 3.0) - lv[j - 1, r, s]
                if not done:
                    lv[j + 1, r, s] = fresh
                if r == 0 and s < 8:
                    here = lv[j, 0, s]
                    level_out[j, s] = here
                    squares = squares + here * here
                    products = products + here * fresh
        part[j : j + 1, :] = jnp.sum(squares, axis=0, keepdims=True)
        part[8 + j : 9 + j, :] = jnp.sum(products, axis=0, keepdims=True)
    sums = jnp.sum(part[...], axis=1, keepdims=True)
    diagonal = lax.broadcasted_iota(jnp.int32, (16, 128), 0) == lax.broadcasted_iota(
        jnp.int32, (16, 128), 1
    )
    one_row = jnp.sum(jnp.where(diagonal, sums, 0.0), axis=0, keepdims=True)
    row_out[...] = jnp.broadcast_to(one_row, row_out.shape)


def combine_kernel(rows, levels, pot, out):
    total = jnp.broadcast_to(jnp.sum(rows[...], axis=0, keepdims=True), (16, 128))
    diagonal = lax.broadcasted_iota(jnp.int32, (16, 128), 0) == lax.broadcasted_iota(
        jnp.int32, (16, 128), 1
    )
    sums = jnp.sum(jnp.where(diagonal, total, 0.0), axis=1, keepdims=True)

    def entry(i):
        return jnp.broadcast_to(sums[i : i + 1, :], TILE)

    moment = [None] * 16
    moment[0], moment[1] = entry(0), entry(8)
    for k in range(1, ITERS):
        moment[2 * k] = 2.0 * entry(k) - moment[0]
        moment[2 * k + 1] = 2.0 * entry(8 + k) - moment[1]
    gram = {}
    for i in range(ITERS + 1):
        for j in range(i, ITERS + 1):
            if i + j < 16:
                gram[i, j] = gram[j, i] = 0.5 * (moment[i + j] + moment[j - i])

    def add_up(terms):
        while len(terms) > 1:
            terms = [
                terms[i] + terms[i + 1] if i + 1 < len(terms) else terms[i]
                for i in range(0, len(terms), 2)
            ]
        return terms[0]

    def inner(a, b):
        return add_up(
            [x * add_up([gram[i, j] * y for j, y in enumerate(b)]) for i, x in enumerate(a)]
        )

    one, zero = jnp.ones(TILE, jnp.float32), jnp.zeros(TILE, jnp.float32)
    search, rest, found = [one], [one], []
    left = moment[0]
    for k in range(ITERS):
        image = [zero] * (k + 2)
        for j in range(k + 1):
            image[j] = image[j] + diag_coef * search[j]
            if j == 0:
                image[1] = image[1] + 6.0 * search[0]
            else:
                image[j + 1] = image[j + 1] + 3.0 * search[j]
                image[j - 1] = image[j - 1] + 3.0 * search[j]
        length = left / inner(search, image)
        found = [
            (found[j] if j < len(found) else zero) + length * search[j] for j in range(k + 1)
        ]
        if k == ITERS - 1:
            break
        rest = [(rest[j] if j < k + 1 else zero) - length * image[j] for j in range(k + 2)]
        fresh = inner(rest, rest)
        ratio = fresh / left
        search = [rest[j] + (ratio * search[j] if j < k + 1 else zero) for j in range(k + 2)]
        left = fresh
    for z in range(8):
        running = found[0] * levels[0, z]
        for j in range(1, ITERS):
            running = running + found[j] * levels[j, z]
        out[z] = pot[z] + running


def in_vmem(count):
    return [pl.BlockSpec(memory_space=pltpu.VMEM)] * count


def f32(*shape):
    return jax.ShapeDtypeStruct(shape, jnp.float32)


def call(kernel, name, outs, scratch, *args, in_specs=None):
    return pl.pallas_call(
        kernel,
        name=name,
        out_shape=outs,
        in_specs=in_specs or in_vmem(len(args)),
        out_specs=in_vmem(len(outs)),
        scratch_shapes=[
            pltpu.VMEM(shape, jnp.float32) if isinstance(shape, tuple) else shape
            for shape in scratch
        ],
        compiler_params=pltpu.CompilerParams(vmem_limit_bytes=48 << 20),
    )(*args)


def send(block, axis, step):
    count = lax.axis_size(axis)
    return lax.ppermute(block, axis, [(i, (i + step) % count) for i in range(count)])


def local(populations, concentrations, potential, solid_mask, surface_sign):
    inputs = tuple(
        pltpu.with_memory_space_constraint(a, pltpu.HBM)
        for a in (populations, concentrations, potential, solid_mask, surface_sign)
    )
    packed = call(
        pack_kernel,
        "pack",
        tuple(jax.ShapeDtypeStruct(a.shape, a.dtype) for a in inputs)
        + (f32(XT, 8, 128), f32(XT, 8, 128), f32(YT, 8, 128), f32(YT, 8, 128)),
        [pltpu.SemaphoreType.DMA((5,))],
        *inputs,
        in_specs=[pl.BlockSpec(memory_space=pltpu.HBM)] * 5,
    )
    kept, (x_left, x_right, y_down, y_up) = packed[:5], packed[5:]
    up = send(y_down, "gy", -1)
    down = send(y_up, "gy", 1)
    from_right = send(x_left, "gx", -1)
    from_left = send(x_right, "gx", 1)
    corner_low, corner_high = call(
        corner_kernel,
        "corners",
        (f32(XT + 1, 8, 128), f32(XT + 1, 8, 128)),
        [],
        from_right,
        from_left,
    )
    corner_up = send(corner_low, "gy", -1)
    corner_down = send(corner_high, "gy", 1)
    relaxed, mask, conc_last, edge = call(
        step_kernel,
        "steps",
        tuple(f32(*shape) for shape in STEP_SHAPES[0]),
        STEP_SHAPES[1],
        *kept,
        x_left,
        x_right,
        down,
        up,
        from_right,
        from_left,
        corner_up,
        corner_down,
    )
    strip = edge[8:]
    left = send(strip, "gx", 1)
    right = send(strip, "gx", -1)
    pop_new, conc_new = call(
        finish_kernel,
        "finish",
        (f32(19, 8, 8, 128), f32(3, 8, 8, 128)),
        [],
        relaxed,
        mask,
        conc_last,
    )
    left, right, pop_new, conc_new = lax.optimization_barrier((left, right, pop_new, conc_new))
    wide = jnp.concatenate([edge, left, right])
    above = send(wide, "gy", -1)
    below = send(wide, "gy", 1)
    devices = lax.axis_size("gx") * lax.axis_size("gy")
    levels, rows = call(
        levels_kernel,
        "levels",
        (f32(ITERS, 8, 8, 128), f32(devices, 128)),
        [(ITERS, 3, 10, 8, 128), (16, 128)],
        edge,
        left,
        right,
        below,
        above,
    )
    rows = lax.all_to_all(rows, ("gx", "gy"), 0, 0, tiled=True)
    (pot_new,) = call(combine_kernel, "combine", (f32(8, 8, 128),), [], rows, levels, kept[2])
    return (pop_new, conc_new, pot_new)


def solution(mesh):
    placed = (
        P(None, None, "gy", "gx"),
        P(None, None, "gy", "gx"),
        P(None, "gy", "gx"),
        P(None, "gy", "gx"),
        P(None, "gy", "gx"),
    )
    return jax.shard_map(
        local,
        mesh=mesh,
        in_specs=placed,
        out_specs=(P(None, None, "gy", "gx"), P(None, None, "gy", "gx"), P(None, "gy", "gx")),
        check_vma=False,
    )
```

```python
import jax
import jax.numpy as jnp
from jax import lax
from jax.experimental import pallas as pl
from jax.experimental.pallas import tpu as pltpu
from jax.sharding import PartitionSpec as P

STEPS = 4
ITERS = 8

lattice_velocity = (
    (0, 0, 0),
    (0, 0, 1),
    (0, 0, -1),
    (0, 1, 0),
    (0, -1, 0),
    (1, 0, 0),
    (-1, 0, 0),
    (0, 1, 1),
    (0, -1, -1),
    (0, 1, -1),
    (0, -1, 1),
    (1, 0, 1),
    (-1, 0, -1),
    (1, 0, -1),
    (-1, 0, 1),
    (1, 1, 0),
    (-1, -1, 0),
    (1, -1, 0),
    (-1, 1, 0),
)
opposite = (0, 2, 1, 4, 3, 6, 5, 8, 7, 10, 9, 12, 11, 14, 13, 16, 15, 18, 17)
lattice_weight = (1.0 / 3.0,) + (1.0 / 18.0,) * 6 + (1.0 / 36.0,) * 12
relax_time = 1.25
force_scale = 0.05
valences = (1.0, -1.0, 2.0)
diffusivity = (0.05, 0.07, 0.03)
diag_coef = 6.0001
surface_scale = 2.0

FIELDS = 25
XT = 7
YT = 97
F_CONC, F_FLUID, F_POT, F_POT2 = 19, 22, 23, 24
SLABS = 9
TILE = (8, 128)


def lane_id():
    return lax.broadcasted_iota(jnp.int32, TILE, 1)


def row_id():
    return lax.broadcasted_iota(jnp.int32, TILE, 0)


def rl(v, amount):
    amount = amount % 128
    return v if amount == 0 else pltpu.roll(v, amount, 1)


def rs(v, amount):
    amount = amount % 8
    return v if amount == 0 else pltpu.roll(v, amount, 0)


def in_lanes(lane, start, width):
    return (lane >= start) & (lane < start + width)


def pack_kernel(
    pop_in, conc_in, pot_in, solid_in, sign_in, pop, conc, pot, solid, sign,
    x_left, x_right, y_down, y_up, sems,
):
    lane, row = lane_id(), row_id()
    top = row < 4
    moves = []
    for i, (source, copy) in enumerate(
        ((pop_in, pop), (conc_in, conc), (pot_in, pot), (solid_in, solid), (sign_in, sign))
    ):
        moves.append(pltpu.make_async_copy(source, copy, sems.at[i]))
    for move in moves:
        move.start()
    for move in moves:
        move.wait()

    def tile(k, z):
        if k < F_CONC:
            return pop[k, z]
        if k < F_FLUID:
            return conc[k - F_CONC, z]
        if k == F_FLUID:
            return 1.0 - solid[z].astype(jnp.float32)
        return pot[z]

    for t in range(XT):
        left = right = jnp.zeros(TILE, jnp.float32)
        for q in range(4):
            k = 4 * t + q
            if k >= FIELDS:
                continue
            inner = 4 if k == F_POT2 else 0
            for z in range(8):
                v = tile(k, z)
                at = 16 * z + 4 * q
                here = in_lanes(lane, at, 4)
                left = jnp.where(here, rl(v, at - inner), left)
                right = jnp.where(here, rl(v, at - (124 - inner)), right)
            if k == F_POT2:
                low, high = tile(k, 0), tile(k, 0)
                low, high = rs(low, -4), rs(high, -3)
                for z in range(1, 8):
                    low = jnp.where(row == z, rs(tile(k, z), z - 4), low)
                    high = jnp.where(row == z, rs(tile(k, z), z - 3), high)
                y_down[4 * k] = low
                y_up[4 * k] = high
                continue
            for pair in range(4):
                a, b = tile(k, 2 * pair), tile(k, 2 * pair + 1)
                y_down[4 * k + pair] = jnp.where(top, a, rs(b, 4))
                y_up[4 * k + pair] = jnp.where(top, rs(a, 4), b)
        x_left[t] = left
        x_right[t] = right


def corner_kernel(right, left, down_out, up_out):
    top = row_id() < 4
    for t in range(XT):
        a, b = right[t], rs(left[t], 4)
        down_out[t] = jnp.where(top, a, b)
        up_out[t] = jnp.where(top, b, a)
    tp = F_POT // 4
    a, b = rs(right[tp], 4), left[tp]
    down_out[XT] = jnp.where(top, a, b)
    up_out[XT] = jnp.where(top, b, a)


def y_shift(a, b, cy, halves=(0, 1)):
    if cy == 0:
        return a, b
    edge = row_id() == (0 if cy > 0 else 7)
    ra, rb = rs(a, cy), rs(b, cy)
    return tuple(jnp.where(edge, rb, ra) if h == 0 else jnp.where(edge, ra, rb) for h in halves)


def x_shift(v, side, z, cx):
    if cx > 0:
        return jnp.where(lane_id() == 0, rl(side, -(16 * z + 3)), rl(v, 1))
    return jnp.where(lane_id() == 127, rl(side, 127 - (16 * z + 12)), rl(v, -1))


def shifted(get, offset, own=False):
    cz, cy, cx = offset
    halves = (0,) if own else (0, 1)
    side = y_shift(get(16), get(17), cy, halves) if cx or not own else None
    out = []
    for z in range(8):
        source = (z - cz) % 8
        v = y_shift(get(2 * source), get(2 * source + 1), cy, halves)
        if cx:
            v = tuple(x_shift(v[h], side[h], source, cx) for h in halves)
        out.append(v)
    if not own:
        out.append(tuple(rl(side[h], 16 * cz + cx) for h in halves))
    return out


def shifted_slab(get, offset, s):
    cz, cy, cx = offset
    if s == 8:
        v = y_shift(get(16), get(17), cy)
        return tuple(rl(x, 16 * cz + cx) for x in v)
    source = (s - cz) % 8
    v = y_shift(get(2 * source), get(2 * source + 1), cy)
    if cx:
        side = y_shift(get(16), get(17), cy)
        v = tuple(x_shift(v[h], side[h], source, cx) for h in range(2))
    return v


def step_kernel(
    pop, conc, pot, solid, sign, x_left, x_right, down, up, from_right, from_left, corner_up,
    corner_down, g, mask, cn, edge_out,
    f, below_rows, vel, cc, fluid, pt, dpot, field, flux,
):
    lane, row = lane_id(), row_id()
    top = row < 4
    slot = lane % 16

    def halves(k, z):
        u, d = up[4 * k + z // 2], down[4 * k + z // 2]
        if z % 2 == 0:
            return jnp.where(top, u, rs(d, 4))
        return jnp.where(top, rs(u, 4), d)

    def strip(k, tiles, low, high):
        q = k % 4
        out = jnp.where(slot < 4, rl(low, -4 * q), rl(high, 12 - 4 * q))
        for z in range(8):
            out = jnp.where(in_lanes(lane, 16 * z + 4, 4), rl(tiles[z], 16 * z + 4), out)
            out = jnp.where(in_lanes(lane, 16 * z + 8, 4), rl(tiles[z], 16 * z + 8 - 124), out)
        return out

    def corners(t):
        u, d = corner_up[t], corner_down[t]
        return rs(jnp.where(top, d, u), 4), jnp.where(top, u, d)

    def strips(k, b):
        t = k // 4
        low, high = corners(t)
        q = k % 4
        mine = jnp.where(
            slot < 8,
            jnp.where(slot < 4, rl(from_left[t], -4 * q), rl(x_left[t], 4 - 4 * q)),
            jnp.where(slot < 12, rl(x_right[t], 8 - 4 * q), rl(from_right[t], 12 - 4 * q)),
        )
        return mine, strip(k, b, low, high)

    def load(k, own, put):
        a = [own(z) for z in range(8)]
        b = [halves(k, z) for z in range(8)]
        for z in range(8):
            put(2 * z, a[z])
            put(2 * z + 1, b[z])
        sa, sb = strips(k, b)
        put(16, sa)
        put(17, sb)

    def putter(ref, *index):
        def put(i, v):
            ref[(*index, i)] = v

        return put

    for k in range(3):
        load(F_CONC + k, lambda z, k=k: conc[k, z], putter(cc, k))
    load(F_FLUID, lambda z: 1.0 - solid[z].astype(jnp.float32), putter(fluid))
    load(F_POT, lambda z: pot[z], putter(pt))

    for i in range(1, 19):
        moved = shifted(lambda s: fluid[s], lattice_velocity[i])
        for s in range(SLABS):
            for h in range(2):
                mask[i - 1, 2 * s + h] = moved[s][h] * fluid[2 * s + h]

    u, d = up[4 * F_POT2], down[4 * F_POT2]
    far = [jnp.where(row == 3, rs(u, 3 - z), rs(d, 4 - z)) for z in range(8)]
    t2, q2 = F_POT2 // 4, F_POT2 % 4
    u, d = corner_up[XT], corner_down[XT]
    far_low = jnp.where(row == 3, rs(u, -1), rs(d, 1))
    far_high = jnp.where(row == 3, rs(u, 3), rs(d, -3))
    far.append(strip(F_POT, far, far_low, far_high))
    low, high = corners(t2)
    edge_low, edge_high = (from_left[t2], low), (from_right[t2], high)
    for axis in range(3):
        plus = tuple(1 if d == axis else 0 for d in range(3))
        minus = tuple(-p for p in plus)
        below = shifted(lambda s: pt[s], plus)
        above = shifted(lambda s: pt[s], minus)
        for s in range(SLABS):
            for h in range(2):
                lo, hi = below[s][h], above[s][h]
                if axis == 1 and h == 1:
                    lo = jnp.where(row == 4, far[s], lo)
                    hi = jnp.where(row == 3, far[s], hi)
                if axis == 2 and s == 8:
                    lo = jnp.where(slot == 0, rl(edge_low[h], -4 * q2 - 3), lo)
                    hi = jnp.where(slot == 15, rl(edge_high[h], 15 - 4 * q2), hi)
                    for z in range(8):
                        hi = jnp.where(lane == 16 * z + 7, rl(pt[2 * z + h], 16 * z + 3), hi)
                here = pt[2 * s + h]
                if h == 0 and s < 8:
                    dpot[3 + axis, 2 * s] = here - lo
                dpot[axis, 2 * s + h] = hi - here
                field[axis, 2 * s + h] = (0.5 * force_scale) * (lo - hi)

    pairs = [(i, i + 1) for i in range(1, 19, 2)]

    def along(c, vector):
        running = None
        for d in range(3):
            if c[d] != 0:
                if running is None:
                    running = vector[d] if c[d] > 0 else -vector[d]
                else:
                    running = running + vector[d] if c[d] > 0 else running - vector[d]
        return running

    def collide(s, v):
        total = {}
        delta = {}
        for a, b in pairs:
            total[a] = v[a] + v[b]
            delta[a] = v[a] - v[b]
        density = (
            v[0]
            + ((total[1] + total[3]) + (total[5] + total[7]))
            + ((total[9] + total[11]) + (total[13] + total[15]) + total[17])
        )
        momentum = (
            (delta[5] + delta[11]) + (delta[13] + delta[15]) + delta[17],
            (delta[3] + delta[7]) + (delta[9] + delta[15]) - delta[17],
            (delta[1] + delta[7]) - (delta[9] - delta[11]) - delta[13],
        )
        open_cell = fluid[s]
        charge = open_cell * (
            valences[0] * cc[0, s] + valences[1] * cc[1, s] + valences[2] * cc[2, s]
        )
        force = [charge * field[d, s] for d in range(3)]
        inverse = 1.0 / density
        u = [(momentum[d] + 0.5 * force[d]) * inverse for d in range(3)]
        for d in range(3):
            vel[d, s] = u[d]
        speed = u[0] * u[0] + u[1] * u[1] + u[2] * u[2]
        work = u[0] * force[0] + u[1] * force[1] + u[2] * force[2]
        flow = [density * u[d] for d in range(3)]
        keep = 1.0 - 1.0 / relax_time
        gain = 1.0 / relax_time
        push = 1.0 - 0.5 / relax_time
        base = gain * density - (1.5 * gain) * (density * speed) - (3.0 * push) * work
        odd = [(3.0 * gain) * flow[d] + (3.0 * push) * force[d] for d in range(3)]
        even = [(4.5 * gain) * flow[d] + (9.0 * push) * force[d] for d in range(3)]
        is_open = open_cell > 0.5
        g[0, s] = jnp.where(is_open, keep * v[0] + lattice_weight[0] * base, v[0])
        for a, b in pairs:
            c, w = lattice_velocity[a], lattice_weight[a]
            middle = base + along(c, u) * along(c, even)
            side = along(c, odd)
            g[a, s] = jnp.where(is_open, keep * v[a] + w * (middle + side), v[b])
            g[b, s] = jnp.where(is_open, keep * v[b] + w * (middle - side), v[a])

    for z in range(8):
        collide(2 * z, [pop[k, z] for k in range(19)])
    for z in range(8):
        v = [halves(k, z) for k in range(19)]
        for k in range(19):
            below_rows[k, z] = v[k]
        collide(2 * z + 1, v)
    both = [
        strips(k, [below_rows[k, z] for z in range(8)])
        for k in range(19)
    ]
    for h in range(2):
        collide(16 + h, [both[k][h] for k in range(19)])

    def stream():
        for s in range(2 * SLABS):
            f[0, s] = g[0, s]
        for s in range(SLABS):
            for i in range(1, 19):
                moved = shifted_slab(lambda n, i=i: g[i, n], lattice_velocity[i], s)
                for h in range(2):
                    n = 2 * s + h
                    f[i, n] = jnp.where(mask[i - 1, n] > 0.5, moved[h], g[opposite[i], n])
        for s in range(2 * SLABS):
            collide(s, [f[i, s] for i in range(19)])

    def ions(own=False):
        for axis in range(3):
            plus = tuple(1 if d == axis else 0 for d in range(3))
            minus = tuple(-p for p in plus)
            upper = 2 * (2 - axis) + 1
            for s in [8] + list(range(8)):
                v_high = shifted_slab(lambda n: vel[axis, n], minus, s)
                c_high = [shifted_slab(lambda n, k=k: cc[k, n], minus, s) for k in range(3)]
                for h in range(2):
                    n = 2 * s + h
                    speed = 0.25 * (vel[axis, n] + v_high[h])
                    step, is_open = dpot[axis, n], mask[upper, n]
                    for k in range(3):
                        rate = diffusivity[k]
                        here, hi = cc[k, n], c_high[k][h]
                        pull = speed - (0.5 * rate * valences[k]) * step
                        flux[axis, k, n] = is_open * (rate * (here - hi) + (here + hi) * pull)
        for k in range(3):
            for s in range(8 if own else SLABS):
                low = [
                    shifted_slab(
                        lambda n, d=d: flux[d, k, n], tuple(1 if e == d else 0 for e in range(3)), s
                    )
                    for d in range(3)
                ]
                for h in range(1 if own else 2):
                    n = 2 * s + h
                    net = [flux[d, k, n] - low[d][h] for d in range(3)]
                    cn[k, n] = cc[k, n] - ((net[0] + net[1]) + net[2])

    def one_step(step, carry):
        ions()
        for k in range(3):
            for n in range(2 * SLABS):
                cc[k, n] = cn[k, n]
        stream()
        return carry

    lax.fori_loop(0, STEPS - 1, one_step, 0)
    ions(own=True)

    edge = jnp.zeros(TILE, jnp.float32)
    for z in range(8):
        n = 2 * z
        c = [cn[k, n] for k in range(3)]
        open_cell = fluid[n]
        target = open_cell * (
            valences[0] * c[0] + valences[1] * c[1] + valences[2] * c[2]
        ) + surface_scale * sign[z].astype(jnp.float32) * (1.0 - open_cell)
        spread = (
            (dpot[0, n] - dpot[3, n]) + (dpot[1, n] - dpot[4, n]) + (dpot[2, n] - dpot[5, n])
        )
        residual = target - ((diag_coef - 6.0) * pt[n] - spread)
        edge_out[z] = residual
        edge = jnp.where(in_lanes(lane, 16 * z, 8), rl(residual, 16 * z - 120), edge)
        edge = jnp.where(in_lanes(lane, 16 * z + 8, 8), rl(residual, 16 * z + 8), edge)
    edge_out[8] = edge


STEP_SHAPES = (
    (
        (19, 2 * SLABS, 8, 128),
        (18, 2 * SLABS, 8, 128),
        (3, 2 * SLABS, 8, 128),
        (9, 8, 128),
    ),
    (
        (19, 2 * SLABS, 8, 128),
        (19, 8, 8, 128),
        (3, 2 * SLABS, 8, 128),
        (3, 2 * SLABS, 8, 128),
        (2 * SLABS, 8, 128),
        (2 * SLABS, 8, 128),
        (6, 2 * SLABS, 8, 128),
        (3, 2 * SLABS, 8, 128),
        (3, 3, 2 * SLABS, 8, 128),
    ),
)


def finish_kernel(g, mask, conc, pop_out, conc_out):
    for z in range(8):
        for k in range(3):
            conc_out[k, z] = conc[k, 2 * z]
        pop_out[0, z] = g[0, 2 * z]
    for i in range(1, 19):
        moved = shifted(lambda s, i=i: g[i, s], lattice_velocity[i], own=True)
        for z in range(8):
            pop_out[i, z] = jnp.where(
                mask[i - 1, 2 * z] > 0.5, moved[z][0], g[opposite[i], 2 * z]
            )


def levels_kernel(own, left, right, down, up, level_out, row_out, lv, part):
    lane, row = lane_id(), row_id()
    slot = lane % 16
    first_row, last_row = row == 0, row == 7
    first_lane, last_lane = lane == 0, lane == 127
    sources = (
        (own, left[0], right[0]),
        (up, up[10], up[9]),
        (down, down[10], down[9]),
    )
    for r, (main, low, high) in enumerate(sources):
        for s in range(8):
            lv[0, r, s] = main[s]
        lv[0, r, 8] = jnp.where(slot < 8, low, main[8])
        lv[0, r, 9] = jnp.where(slot < 8, main[8], high)

    def around(j, r, s, low, high):
        v = lv[j, r, s]
        above, below = lv[j, (r + 1) % 3, s], lv[j, (r + 2) % 3, s]
        vertical = jnp.where(last_row, rs(above, -1), rs(v, -1)) + jnp.where(
            first_row, rs(below, 1), rs(v, 1)
        )
        if s < 8:
            across = jnp.where(first_lane, rl(low, -(16 * s + 7)), rl(v, 1)) + jnp.where(
                last_lane, rl(high, 127 - (16 * s + 8)), rl(v, -1)
            )
            return (lv[j, r, (s + 1) % 8] + lv[j, r, (s - 1) % 8]) + vertical + across
        return (rl(v, 16) + rl(v, -16)) + vertical + (rl(v, 1) + rl(v, -1))

    for j in range(ITERS):
        done = j == ITERS - 1
        squares = products = jnp.zeros(TILE, jnp.float32)
        for r in range(1 if done else 3):
            low, high = lv[j, r, 8], lv[j, r, 9]
            for s in range(8 if done else 10):
                total = around(j, r, s, low, high)
                if j == 0:
                    fresh = -total / 6.0
                else:
                    fresh = total * (-1.0 / 3.0) - lv[j - 1, r, s]
                if not done:
                    lv[j + 1, r, s] = fresh
                if r == 0 and s < 8:
                    here = lv[j, 0, s]
                    level_out[j, s] = here
                    squares = squares + here * here
                    products = products + here * fresh
        part[j : j + 1, :] = jnp.sum(squares, axis=0, keepdims=True)
        part[8 + j : 9 + j, :] = jnp.sum(products, axis=0, keepdims=True)
    sums = jnp.sum(part[...], axis=1, keepdims=True)
    diagonal = lax.broadcasted_iota(jnp.int32, (16, 128), 0) == lax.broadcasted_iota(
        jnp.int32, (16, 128), 1
    )
    one_row = jnp.sum(jnp.where(diagonal, sums, 0.0), axis=0, keepdims=True)
    row_out[...] = jnp.broadcast_to(one_row, row_out.shape)


def combine_kernel(rows, levels, pot, out):
    total = jnp.broadcast_to(jnp.sum(rows[...], axis=0, keepdims=True), (16, 128))
    diagonal = lax.broadcasted_iota(jnp.int32, (16, 128), 0) == lax.broadcasted_iota(
        jnp.int32, (16, 128), 1
    )
    sums = jnp.sum(jnp.where(diagonal, total, 0.0), axis=1, keepdims=True)

    def entry(i):
        return jnp.broadcast_to(sums[i : i + 1, :], TILE)

    moment = [None] * 16
    moment[0], moment[1] = entry(0), entry(8)
    for k in range(1, ITERS):
        moment[2 * k] = 2.0 * entry(k) - moment[0]
        moment[2 * k + 1] = 2.0 * entry(8 + k) - moment[1]
    gram = {}
    for i in range(ITERS + 1):
        for j in range(i, ITERS + 1):
            if i + j < 16:
                gram[i, j] = gram[j, i] = 0.5 * (moment[i + j] + moment[j - i])

    def add_up(terms):
        while len(terms) > 1:
            terms = [
                terms[i] + terms[i + 1] if i + 1 < len(terms) else terms[i]
                for i in range(0, len(terms), 2)
            ]
        return terms[0]

    def inner(a, b):
        return add_up(
            [x * add_up([gram[i, j] * y for j, y in enumerate(b)]) for i, x in enumerate(a)]
        )

    one, zero = jnp.ones(TILE, jnp.float32), jnp.zeros(TILE, jnp.float32)
    search, rest, found = [one], [one], []
    left = moment[0]
    for k in range(ITERS):
        image = [zero] * (k + 2)
        for j in range(k + 1):
            image[j] = image[j] + diag_coef * search[j]
            if j == 0:
                image[1] = image[1] + 6.0 * search[0]
            else:
                image[j + 1] = image[j + 1] + 3.0 * search[j]
                image[j - 1] = image[j - 1] + 3.0 * search[j]
        length = left / inner(search, image)
        found = [
            (found[j] if j < len(found) else zero) + length * search[j] for j in range(k + 1)
        ]
        if k == ITERS - 1:
            break
        rest = [(rest[j] if j < k + 1 else zero) - length * image[j] for j in range(k + 2)]
        fresh = inner(rest, rest)
        ratio = fresh / left
        search = [rest[j] + (ratio * search[j] if j < k + 1 else zero) for j in range(k + 2)]
        left = fresh
    for z in range(8):
        running = found[0] * levels[0, z]
        for j in range(1, ITERS):
            running = running + found[j] * levels[j, z]
        out[z] = pot[z] + running


def in_vmem(count):
    return [pl.BlockSpec(memory_space=pltpu.VMEM)] * count


def f32(*shape):
    return jax.ShapeDtypeStruct(shape, jnp.float32)


def call(kernel, name, outs, scratch, *args, in_specs=None):
    return pl.pallas_call(
        kernel,
        name=name,
        out_shape=outs,
        in_specs=in_specs or in_vmem(len(args)),
        out_specs=in_vmem(len(outs)),
        scratch_shapes=[
            pltpu.VMEM(shape, jnp.float32) if isinstance(shape, tuple) else shape
            for shape in scratch
        ],
        compiler_params=pltpu.CompilerParams(vmem_limit_bytes=48 << 20),
    )(*args)


def send(block, axis, step):
    count = lax.axis_size(axis)
    return lax.ppermute(block, axis, [(i, (i + step) % count) for i in range(count)])


def local(populations, concentrations, potential, solid_mask, surface_sign):
    inputs = tuple(
        pltpu.with_memory_space_constraint(a, pltpu.HBM)
        for a in (populations, concentrations, potential, solid_mask, surface_sign)
    )
    packed = call(
        pack_kernel,
        "pack",
        tuple(jax.ShapeDtypeStruct(a.shape, a.dtype) for a in inputs)
        + (f32(XT, 8, 128), f32(XT, 8, 128), f32(YT, 8, 128), f32(YT, 8, 128)),
        [pltpu.SemaphoreType.DMA((5,))],
        *inputs,
        in_specs=[pl.BlockSpec(memory_space=pltpu.HBM)] * 5,
    )
    kept, (x_left, x_right, y_down, y_up) = packed[:5], packed[5:]
    up = send(y_down, "gy", -1)
    down = send(y_up, "gy", 1)
    from_right = send(x_left, "gx", -1)
    from_left = send(x_right, "gx", 1)
    corner_low, corner_high = call(
        corner_kernel,
        "corners",
        (f32(XT + 1, 8, 128), f32(XT + 1, 8, 128)),
        [],
        from_right,
        from_left,
    )
    corner_up = send(corner_low, "gy", -1)
    corner_down = send(corner_high, "gy", 1)
    relaxed, mask, conc_last, edge = call(
        step_kernel,
        "steps",
        tuple(f32(*shape) for shape in STEP_SHAPES[0]),
        STEP_SHAPES[1],
        *kept,
        x_left,
        x_right,
        down,
        up,
        from_right,
        from_left,
        corner_up,
        corner_down,
    )
    strip = edge[8:]
    right = send(strip, "gx", -1)
    left = send(strip, "gx", 1)
    pop_new, conc_new = call(
        finish_kernel,
        "finish",
        (f32(19, 8, 8, 128), f32(3, 8, 8, 128)),
        [],
        relaxed,
        mask,
        conc_last,
    )
    right, left, pop_new, conc_new = lax.optimization_barrier((right, left, pop_new, conc_new))
    wide = jnp.concatenate([edge, right, left])
    above = send(wide, "gy", -1)
    below = send(wide, "gy", 1)
    devices = lax.axis_size("gx") * lax.axis_size("gy")
    levels, rows = call(
        levels_kernel,
        "levels",
        (f32(ITERS, 8, 8, 128), f32(devices, 128)),
        [(ITERS, 3, 10, 8, 128), (16, 128)],
        edge,
        left,
        right,
        below,
        above,
    )
    rows = lax.all_to_all(rows, ("gx", "gy"), 0, 0, tiled=True)
    (pot_new,) = call(combine_kernel, "combine", (f32(8, 8, 128),), [], rows, levels, kept[2])
    return (pop_new, conc_new, pot_new)


def solution(mesh):
    placed = (
        P(None, None, "gy", "gx"),
        P(None, None, "gy", "gx"),
        P(None, "gy", "gx"),
        P(None, "gy", "gx"),
        P(None, "gy", "gx"),
    )
    return jax.shard_map(
        local,
        mesh=mesh,
        in_specs=placed,
        out_specs=(P(None, None, "gy", "gx"), P(None, None, "gy", "gx"), P(None, "gy", "gx")),
        check_vma=False,
    )
```
